32 devices in a mesh: row: 16 (over z, x, core), chan: 2 (over y).
Axes of the slice: x: 2, y: 2, z: 4, core: 2. Of those that a mesh axis runs over, the one named last changes fastest.
Arguments:
- sky_image: float32 [2, 4096, 4096], P('chan', 'row'), may hold values from -6 to 6
- fourier_dual: float32 [2, 2, 4096, 4096], P(None, 'chan', 'row'), may hold values from -6 to 6
- visibilities: float32 [2, 2, 4096, 4096], P(None, 'chan', 'row'), may hold values from -18 to 18
- weights: float32 [2, 4096, 4096], P('chan', 'row'), may hold values from 0.1 to 1
- radius: float32 [2], P('chan'), may hold values from 0.2 to 0.6
- wavelet_dual: float32 [2, 4096, 4096], P(None, ('row', 'chan')), may hold values from -6 to 6
- reweight: float32 [4096, 4096], P(('row', 'chan')), may hold values from 0.3 to 3
Outputs:
- image_new: float32 [2, 4096, 4096], P('chan', 'row')
- fourier_new: float32 [2, 2, 4096, 4096], P(None, 'chan', 'row')
- wavelet_new: float32 [2, 4096, 4096], P(None, ('row', 'chan'))
The draws below stay inside these ranges and needn't reach their ends.
All inputs are finite; a program needn't handle non-finite values.
Results may differ from the reference program's by a relative error of at most 0.000084.
Values sent between devices are 32-bit elements; how exact they have to be, the bound alone decides.
No kernel may reach another device: no remote copies, remote signals or barrier semaphores. Data moves between devices by JAX's collectives and lax.ppermute only.
A program may use at most 192 MiB of HBM per device.

```python
import math
import jax
import jax.numpy as jnp
from jax import lax

N = 4096
C = 2


def draw_visibilities(key, part):
    array_shape = (2, C, N, N)
    fraction = jnp.arange(N, dtype=jnp.float32) / (N - 1)
    entries = jax.random.truncated_normal(key, -6.0, 6.0, array_shape, jnp.float32)
    row_scale = 1.0 + 2.0 * fraction
    return entries * row_scale[None, None, :, None]


def block_scale(own_key, extent, cuts, least, largest):
    def one(position, shards_of):
        draws = jax.random.uniform(jax.random.fold_in(jax.random.fold_in(own_key, 6), position), (shards_of,), jnp.float32, least / len(cuts), largest / len(cuts))
        return jnp.repeat(jnp.exp(draws), extent[position] // shards_of).reshape((-1,) + (1,) * (len(extent) - position - 1))

    factor_of = one(*cuts[0])
    for cut in cuts[1:]:
        factor_of = factor_of * one(*cut)
    return factor_of


def scatter_about(key, dims, deviation, reach, shards=(), held_as=jnp.bfloat16):
    values = deviation * jax.random.normal(key, dims, jnp.float32)
    if shards:
        values = values * block_scale(key, dims, shards, -0.22, 0.18)
    return jnp.clip(values, -reach, reach).astype(held_as)


def setup_inputs(seed: int = 0) -> dict:
    keys = jax.random.split(jax.random.key(seed), 8)
    return {
        "sky_image": scatter_about(keys[0], (C, N, N), 1.0, 6.0, ((0, 2), (1, 16)), jnp.float32),
        "fourier_dual": scatter_about(keys[1], (2, C, N, N), 1.0, 6.0, ((1, 2), (2, 16)), jnp.float32),
        "visibilities": draw_visibilities(jax.random.fold_in(keys[7], 71), 0),
        "weights": jnp.clip(jnp.exp(math.log(1.0) - 2.3025851 * jax.random.uniform(keys[3], (C, N, N), jnp.float32) ** block_scale(keys[3], (C, N, N), ((0, 2), (1, 16)), -0.2, 0.2)), 0.1, 1.0),
        "radius": jnp.clip(0.2 + 0.400000021 * jax.random.uniform(keys[4], (C,), jnp.float32) ** block_scale(keys[4], (C,), ((0, 2),), -0.2, 0.2), 0.2, 0.6),
        "wavelet_dual": scatter_about(keys[5], (C, N, N), 1.0, 6.0, ((1, 32),), jnp.float32),
        "reweight": jnp.clip(jnp.exp(math.log(3.0) - 2.3025851 * jax.random.uniform(keys[6], (N, N), jnp.float32) ** block_scale(keys[6], (N, N), ((0, 32),), -0.2, 0.2)), 0.3, 3.0),
    }


data_step = 0.8
primal_step = 0.5
low_taps = (0.0625, 0.25, 0.375, 0.25, 0.0625)
high_taps = (-0.1, -0.3, 0.7, -0.2, -0.1)
low_reverse = (0.0625, 0.25, 0.375, 0.25, 0.0625)
high_reverse = (-0.1, -0.2, 0.7, -0.3, -0.1)

def filter_rows(extended, filter_taps):
    count_rows = extended.shape[1] - 4
    total = filter_taps[0] * extended[:, 0:count_rows]
    for offset in range(1, 5):
        total = total + filter_taps[offset] * extended[:, offset:offset + count_rows]
    return total

def filter_columns(values, filter_taps):
    count_cols = values.shape[2]
    padded = jnp.pad(values, ((0, 0), (0, 0), (2, 2)))
    total = filter_taps[0] * padded[:, :, 0:count_cols]
    for offset in range(1, 5):
        total = total + filter_taps[offset] * padded[:, :, offset:offset + count_cols]
    return total

def analysis(extended, low_set, high_set):
    return filter_columns(filter_rows(extended, high_set), low_set) + filter_columns(filter_rows(extended, low_set), high_set)

def soft_dual(combined, threshold):
    magnitude = jnp.sqrt(lax.optimization_barrier(jnp.sum(combined * combined, axis=0)))
    return combined * (threshold / jnp.maximum(magnitude, threshold))

def reference(sky_image, fourier_dual, visibilities, weights, radius, wavelet_dual, reweight):
    side = sky_image.shape[1]
    spectrum = jnp.swapaxes(jnp.fft.fft2(sky_image), 1, 2) / side
    resid_re = fourier_dual[0] / data_step + weights * jnp.real(spectrum) - visibilities[0]
    resid_im = fourier_dual[1] / data_step + weights * jnp.imag(spectrum) - visibilities[1]
    resid_norm = lax.optimization_barrier(jnp.sum(resid_re * resid_re + resid_im * resid_im, axis=(1, 2)))
    data_norm = lax.optimization_barrier(jnp.sum(visibilities[0] * visibilities[0] + visibilities[1] * visibilities[1], axis=(1, 2)))
    shrink = data_step * (1.0 - radius * jnp.sqrt(data_norm) / jnp.sqrt(resid_norm))
    new_re = resid_re * shrink[:, None, None]
    new_im = resid_im * shrink[:, None, None]
    fourier_new = jnp.stack([new_re, new_im])
    weighted = lax.complex(weights * new_re, weights * new_im)
    gradient = jnp.real(jnp.fft.ifft2(jnp.swapaxes(weighted, 1, 2))) * side
    extended = jnp.pad(sky_image, ((0, 0), (2, 2), (0, 0)))
    combined = wavelet_dual + analysis(extended, low_taps, high_taps)
    wavelet_new = soft_dual(combined, reweight)
    adjoint = analysis(jnp.pad(wavelet_new, ((0, 0), (2, 2), (0, 0))), low_reverse, high_reverse)
    image_new = jnp.maximum(sky_image - primal_step * (gradient + adjoint), 0.0)
    return (image_new, fourier_new, wavelet_new)
```

```python
import math
from functools import partial

import jax
import jax.numpy as jnp
import ml_dtypes
import numpy as np
from jax import lax
from jax.experimental import pallas as pl
from jax.experimental.pallas import tpu as pltpu
from jax.sharding import PartitionSpec as P

data_step = 0.8
primal_step = 0.5
low_taps = (0.0625, 0.25, 0.375, 0.25, 0.0625)
high_taps = (-0.1, -0.3, 0.7, -0.2, -0.1)
low_reverse = (0.0625, 0.25, 0.375, 0.25, 0.0625)
high_reverse = (-0.1, -0.2, 0.7, -0.3, -0.1)

VMEM_LIMIT = 60 * 1024 * 1024


def padded_2(array, sides, width):
    for axis, dim in sides:
        count, length = (lax.axis_size(axis), array.shape[dim])
        up = [(i, (i + 1) % count) for i in range(count - 1)]
        down = [(j, i) for i, j in up]
        last = lax.slice_in_dim(array, length - width, length, axis=dim)
        first = lax.slice_in_dim(array, 0, width, axis=dim)
        before = lax.ppermute(last, axis, up)
        after = lax.ppermute(first, axis, down)
        array = jnp.concatenate([before, array, after], axis=dim)
    return array


def filter_rows(extended, filter_taps):
    count_rows = extended.shape[1] - 4
    total = filter_taps[0] * extended[:, 0:count_rows]
    for offset in range(1, 5):
        total = total + filter_taps[offset] * extended[:, offset : offset + count_rows]
    return total


def filter_columns(values, filter_taps):
    count_cols = values.shape[2]
    padded = jnp.pad(values, ((0, 0), (0, 0), (2, 2)))
    total = filter_taps[0] * padded[:, :, 0:count_cols]
    for offset in range(1, 5):
        total = total + filter_taps[offset] * padded[:, :, offset : offset + count_cols]
    return total


def analysis(extended, low_set, high_set):
    return filter_columns(filter_rows(extended, high_set), low_set) + filter_columns(
        filter_rows(extended, low_set), high_set
    )


def soft_dual(combined, threshold):
    magnitude = jnp.sqrt(jnp.sum(combined * combined, axis=0))
    return combined * (threshold / jnp.maximum(magnitude, threshold))


def c_add(x, y):
    if x[1] is None and y[1] is None:
        return (x[0] + y[0], None)
    if x[1] is None:
        return (x[0] + y[0], y[1])
    if y[1] is None:
        return (x[0] + y[0], x[1])
    return (x[0] + y[0], x[1] + y[1])


def c_sub(x, y):
    if x[1] is None and y[1] is None:
        return (x[0] - y[0], None)
    if x[1] is None:
        return (x[0] - y[0], -y[1])
    if y[1] is None:
        return (x[0] - y[0], x[1])
    return (x[0] - y[0], x[1] - y[1])


def c_rot(x, turn):
    turn = turn % 1.0
    wr, wi = math.cos(2 * math.pi * turn), math.sin(2 * math.pi * turn)
    re, im = x
    if turn == 0.0:
        return x
    if turn == 0.5:
        return (-re, None if im is None else -im)
    if turn == 0.25:
        return (jnp.zeros_like(re) if im is None else -im, re)
    if turn == 0.75:
        return (jnp.zeros_like(re) if im is None else im, -re)
    if im is None:
        return (re * wr, re * wi)
    if abs(abs(wr) - abs(wi)) < 1e-12:
        h = abs(wr)
        p, m = (re + im) * h, (re - im) * h
        if wr > 0:
            return (m, p) if wi > 0 else (p, -m)
        return (-p, m) if wi > 0 else (-m, -p)
    return (re * wr - im * wi, re * wi + im * wr)


def c_rot90_add(x, y, sign):
    re, im = x
    yr, yi = y
    if yi is not None:
        re = re - yi if sign > 0 else re + yi
    if im is None:
        im = yr if sign > 0 else -yr
    else:
        im = im + yr if sign > 0 else im - yr
    return (re, im)


def small_dft(xs, sign):
    n = len(xs)
    if n == 1:
        return list(xs)
    if n == 2:
        return [c_add(xs[0], xs[1]), c_sub(xs[0], xs[1])]
    if n % 4 == 0:
        parts = [small_dft(xs[r::4], sign) for r in range(4)]
        out = [None] * n
        for k in range(n // 4):
            t = [c_rot(parts[r][k], sign * r * k / n) for r in range(4)]
            s0, s1 = c_add(t[0], t[2]), c_sub(t[0], t[2])
            s2, s3 = c_add(t[1], t[3]), c_sub(t[1], t[3])
            out[k] = c_add(s0, s2)
            out[k + n // 2] = c_sub(s0, s2)
            out[k + n // 4] = c_rot90_add(s1, s3, sign)
            out[k + 3 * n // 4] = c_rot90_add(s1, s3, -sign)
        return out
    even, odd = small_dft(xs[0::2], sign), small_dft(xs[1::2], sign)
    out = [None] * n
    for k in range(n // 2):
        t = c_rot(odd[k], sign * k / n)
        out[k], out[k + n // 2] = c_add(even[k], t), c_sub(even[k], t)
    return out


def split_constant(table):
    high = table.astype(ml_dtypes.bfloat16)
    low = (table - high.astype(np.float64)).astype(ml_dtypes.bfloat16)
    return high, low


def dft_matrix(rows, cols, length, sign):
    angle = 2.0 * np.pi * ((np.asarray(rows)[:, None] * np.asarray(cols)[None, :]) % length) / length
    return np.cos(angle), sign * np.sin(angle)


def phase_rows(count, positions, length, sign):
    re, im = dft_matrix(np.arange(count), positions, length, sign)
    wide = lambda t: np.ascontiguousarray(np.broadcast_to(t[:, None, :], (count, 8, t.shape[1]))).astype(np.float32)
    return wide(re), wide(im)


def split_value(value):
    high = value.astype(jnp.bfloat16)
    low = (value - high.astype(jnp.float32)).astype(jnp.bfloat16)
    return high, low


def dot_nt(a, b):
    return lax.dot_general(a, b, (((1,), (1,)), ((), ())), preferred_element_type=jnp.float32)


def dot_split(high, low, value):
    v_high, v_low = split_value(value)
    return dot_nt(high, v_high) + (dot_nt(low, v_high) + dot_nt(high, v_low))


def lane_step(width):
    return 128 if width % 128 == 0 else width


def radix_stage(load, tw_re, tw_im, store, rows, width, count, sign):
    step = lane_step(width)

    def body(i, carry):
        at = pl.ds(pl.multiple_of(i * 8, 8), 8)
        for lane in range(0, width, step):
            lanes = slice(lane, lane + step)
            ys = small_dft([load(p, at, lanes) for p in range(count)], sign)
            for p in range(count):
                re, im = ys[p]
                if p == 0:
                    store(p, at, lanes, re, jnp.zeros_like(re) if im is None else im)
                    continue
                wr, wi = tw_re[p, :, lanes], tw_im[p, :, lanes]
                if im is None:
                    store(p, at, lanes, re * wr, re * wi)
                else:
                    store(p, at, lanes, re * wr - im * wi, re * wi + im * wr)
        return carry

    lax.fori_loop(0, rows // 8, body, 0)


def lane_tiles(width):
    step = lane_step(width)
    return width // step, step


def store_rows(out, lead, p, n, count, value):
    tiles, step = lane_tiles(value.shape[1])
    room = out.shape[-1]
    for t in range(tiles):
        piece = value[:, t * step : (t + 1) * step]
        if room > step:
            piece = jnp.concatenate([piece, jnp.zeros((n, room - step), piece.dtype)], axis=1)
        at = pl.ds(p, n, stride=count) if n > 1 else pl.ds(p, 1)
        out[(*lead, t, at, slice(None))] = piece


def mix_pair(f_high, f_low, y_re, y_im, half):
    a = dot_split(f_high[...], f_low[...], y_re)
    b = dot_split(f_high[...], f_low[...], y_im)
    return a[:half] - b[half:], b[:half] + a[half:]


def first_kernel(count, width, kept, x, tw_re, tw_im, f_high, f_low, out, y_re, y_im):
    rows = x.shape[0]

    def load(p, at, lanes):
        return (x[at, p * width + lanes.start : p * width + lanes.stop], None)

    def store(p, at, lanes, re, im):
        y_re[p, at, lanes] = re
        y_im[p, at, lanes] = im

    radix_stage(load, tw_re, tw_im, store, rows, width, count, -1)

    def body(p, carry):
        z_re, z_im = mix_pair(f_high, f_low, y_re[p], y_im[p], count * kept)
        for m in range(count):
            store_rows(out, (m, 0), p, kept, count, z_re[m * kept : (m + 1) * kept])
            store_rows(out, (m, 1), p, kept, count, z_im[m * kept : (m + 1) * kept])
        return carry

    lax.fori_loop(0, count, body, 0)


def flipped(ref, at, n):
    return jnp.concatenate([ref[t, at, :].T for t in range(ref.shape[0])], axis=0)[:n]


def middle_kernel(
    count, width, got, dual, vis, weights, tw_re, tw_im, f_high, f_low, tv_re, tv_im, g_high, g_low,
    resid, out, sums, y_re, y_im, zt_re, zt_im, s_re, s_im,
):
    batch = got.shape[3]
    length = count * width
    per = width // count

    def load(p, at, lanes):
        tile = lanes.start // got.shape[4]
        return (got[p, 0, tile, at, :], got[p, 1, tile, at, :])

    def store(p, at, lanes, re, im):
        y_re[p, at, lanes] = re
        y_im[p, at, lanes] = im

    radix_stage(load, tw_re, tw_im, store, batch, width, count, -1)

    def forward(p, carry):
        z_re, z_im = mix_pair(f_high, f_low, y_re[p], y_im[p], width)
        store_rows(zt_re, (), p, width, count, z_re)
        store_rows(zt_im, (), p, width, count, z_im)
        return carry

    lax.fori_loop(0, count, forward, 0)

    def residual(i, carry):
        d_sum, v_sum = carry
        start = pl.multiple_of(i * 128, 128)
        at = pl.ds(start, 128)
        w = weights[0, :, at]
        v_re, v_im = vis[0, 0, :, at], vis[1, 0, :, at]
        d_re = dual[0, 0, :, at] * (1.0 / data_step) + w * flipped(zt_re, at, batch) - v_re
        d_im = dual[1, 0, :, at] * (1.0 / data_step) + w * flipped(zt_im, at, batch) - v_im
        resid[0, 0, :, at] = d_re
        resid[1, 0, :, at] = d_im
        s_re[:, at] = w * d_re
        s_im[:, at] = w * d_im
        fold = lambda t: jnp.sum(t.reshape(batch // 8, 8, 128), axis=0)
        return d_sum + fold(d_re * d_re + d_im * d_im), v_sum + fold(v_re * v_re + v_im * v_im)

    zero = jnp.zeros((8, 128), jnp.float32)
    d_sum, v_sum = lax.fori_loop(0, length // 128, residual, (zero, zero))
    sums[0] = d_sum
    sums[1] = v_sum

    def load_2(p, at, lanes):
        lanes = slice(p * width + lanes.start, p * width + lanes.stop)
        return (s_re[at, lanes], s_im[at, lanes])

    radix_stage(load_2, tv_re, tv_im, store, batch, width, count, 1)

    def inverse(p, carry):
        u_re, u_im = mix_pair(g_high, g_low, y_re[p], y_im[p], width)
        for m in range(count):
            store_rows(out, (m, 0), p, per, count, u_re[m * per : (m + 1) * per])
            store_rows(out, (m, 1), p, per, count, u_im[m * per : (m + 1) * per])
        return carry

    lax.fori_loop(0, count, inverse, 0)


def last_kernel(count, width, final, has_part, *refs):
    refs = list(refs)
    got, tw_re, tw_im, e_high, e_low = refs[:5]
    refs = refs[5:]
    part = refs.pop(0) if has_part else None
    if final:
        sky, adjoint, shrink, out, y_re, y_im, gt = refs
    else:
        out, y_re, y_im = refs
    rows, batch = got.shape[3], got.shape[2] * got.shape[4]
    length = count * width

    def load(p, at, lanes):
        tile = lanes.start // got.shape[4]
        return (got[p, 0, tile, at, :], got[p, 1, tile, at, :])

    def store(p, at, lanes, re, im):
        y_re[p, at, lanes] = re
        y_im[p, at, lanes] = im

    radix_stage(load, tw_re, tw_im, store, rows, batch, count, 1)

    def inverse(p, carry):
        u = dot_split(e_high[...], e_low[...], jnp.concatenate([y_re[p], y_im[p]], axis=1))
        if has_part:
            u = u + part[p]
        if final:
            store_rows(gt, (), p, width, count, u)
        else:
            out[p] = u
        return carry

    lax.fori_loop(0, count, inverse, 0)
    if final:
        scale = primal_step * shrink[0]

        def finish(i, carry):
            at = pl.ds(pl.multiple_of(i * 128, 128), 128)
            value = sky[:, at] - (scale * flipped(gt, at, rows) + primal_step * adjoint[:, at])
            out[:, at] = jnp.maximum(value, 0.0)
            return carry

        lax.fori_loop(0, length // 128, finish, 0)


def vmem(shape, dtype=jnp.float32):
    return pltpu.VMEM(shape, dtype)


def whole(shape):
    return pl.BlockSpec(shape, lambda *_: (0,) * len(shape), pipeline_mode=pl.Buffered(1))


def call(kernel, args, specs, out_shape, out_specs, scratch, name, flops, moved):
    return pl.pallas_call(
        kernel,
        grid=(1,),
        in_specs=specs,
        out_specs=out_specs,
        out_shape=out_shape,
        scratch_shapes=scratch,
        name=name,
        cost_estimate=pl.CostEstimate(flops=flops, bytes_accessed=moved, transcendentals=0),
        compiler_params=pltpu.CompilerParams(vmem_limit_bytes=VMEM_LIMIT),
    )(*args)


def per_device(sky_image, fourier_dual, visibilities, weights, radius, wavelet_dual, reweight):
    f32 = jnp.float32
    sky = sky_image[0]
    rows, length = sky.shape
    count = lax.axis_size("row")
    width = length // count
    per = width // count
    chunks = 2 if per % 2 == 0 else 1
    batch = width // chunks
    kept = per // chunks
    scale = 1.0 / math.sqrt(length)
    shape = jax.ShapeDtypeStruct

    def tile(high, wide):
        tiles, step = lane_tiles(wide)
        return tiles, high, step

    lanes = np.arange(width)
    tw = phase_rows(count, lanes, length, -1)
    tv = phase_rows(count, lanes, length, 1)
    f_table = split_constant(scale * np.concatenate(dft_matrix(lanes, lanes, width, -1)))
    g_table = split_constant(scale * np.concatenate(dft_matrix(lanes, lanes, width, 1)))

    sent = []
    for c in range(chunks):
        picked = (np.arange(count)[:, None] * per + c * kept + np.arange(kept)[None, :]).reshape(-1)
        table = split_constant(scale * np.concatenate(dft_matrix(picked, lanes, width, -1)))
        args = (sky, *tw, *table)
        piece = call(
            partial(first_kernel, count, width, kept), args, [whole(a.shape) for a in args],
            shape((count, 2, *tile(batch, rows)), f32), whole((count, 2, *tile(batch, rows))),
            [vmem((count, rows, width))] * 2, "first", 10**10, 10**7,
        )
        sent.append(lax.all_to_all(piece, "row", split_axis=0, concat_axis=0, tiled=True))

    facet_image = lax.all_to_all(sky_image, "chan", split_axis=1, concat_axis=0, tiled=True)
    extended = padded_2(facet_image, ((("row", "chan"), 1),), 2)
    combined = wavelet_dual + analysis(extended, low_taps, high_taps)
    wavelet_new = soft_dual(combined, reweight)
    extended_dual = padded_2(wavelet_new, ((("row", "chan"), 1),), 2)
    adjoint = analysis(extended_dual, low_reverse, high_reverse)
    adjoint_rows = lax.all_to_all(adjoint, "chan", split_axis=0, concat_axis=1, tiled=True)

    resid, returned, sums = [], [], 0.0
    for c in range(chunks):
        block = lambda lead, c=c: pl.BlockSpec(
            (*lead, batch, length), lambda i: (0,) * len(lead) + (c, 0), pipeline_mode=pl.Buffered(1)
        )
        tables = (*tw, *f_table, *tv, *g_table)
        outs = (
            shape((2, 1, batch, length), f32),
            shape((count, 2, *tile(rows, batch)), f32),
            shape((2, 8, 128), f32),
        )
        d, piece, part = call(
            partial(middle_kernel, count, width), (sent[c], fourier_dual, visibilities, weights, *tables),
            [whole(sent[c].shape), block((2, 1)), block((2, 1)), block((1,)), *(whole(t.shape) for t in tables)],
            outs, tuple(whole(o.shape) for o in outs),
            [vmem((count, batch, width))] * 2 + [vmem((-(-batch // 128), length, 128))] * 2 + [vmem((batch, length))] * 2,
            "middle", 2 * 10**10, 3 * 10**7,
        )
        resid.append(d)
        sums = sums + part
        returned.append(lax.all_to_all(piece, "row", split_axis=0, concat_axis=0, tiled=True))

    spread = jnp.broadcast_to(sums[None], (count, *sums.shape))
    gathered = lax.all_to_all(spread, "row", split_axis=0, concat_axis=0, tiled=True)
    resid_norm = jnp.sum(gathered[:, 0])
    data_norm = jnp.sum(gathered[:, 1])
    shrink = data_step * (1.0 - radius * jnp.sqrt(data_norm) / jnp.sqrt(resid_norm))
    fourier_new = jnp.concatenate([d * shrink for d in resid], axis=2)

    partial_sum = None
    for c in range(chunks):
        q = c * batch + np.arange(batch)
        phases = phase_rows(count, q, length, 1)
        e_re, e_im = dft_matrix(lanes, q, width, 1)
        table = split_constant(scale * np.concatenate([e_re, -e_im], axis=1))
        final = c == chunks - 1
        args = [returned[c], *phases, *table]
        if partial_sum is not None:
            args.append(partial_sum)
        specs = [whole(a.shape) for a in args]
        scratch = [vmem((count, rows, batch))] * 2
        if final:
            args += [sky, adjoint_rows[0], shrink]
            specs += [whole(sky.shape), whole(sky.shape), pl.BlockSpec(memory_space=pltpu.SMEM)]
            scratch.append(vmem((-(-rows // 128), length, 128)))
            out = shape((rows, length), f32)
        else:
            out = shape((count, width, rows), f32)
        partial_sum = call(
            partial(last_kernel, count, width, final, partial_sum is not None), args, specs,
            out, whole(out.shape), scratch, "last", 10**10, 10**7,
        )
    return (partial_sum[None], fourier_new, wavelet_new)


def solution(mesh):
    in_specs = (
        P("chan", "row", None),
        P(None, "chan", "row", None),
        P(None, "chan", "row", None),
        P("chan", "row", None),
        P("chan"),
        P(None, ("row", "chan"), None),
        P(("row", "chan"), None),
    )
    out_specs = (
        P("chan", "row", None),
        P(None, "chan", "row", None),
        P(None, ("row", "chan"), None),
    )
    return jax.shard_map(
        per_device, mesh=mesh, in_specs=in_specs, out_specs=out_specs, check_vma=False
    )
```

```python
import math
from functools import partial

import jax
import jax.numpy as jnp
import ml_dtypes
import numpy as np
from jax import lax
from jax.experimental import pallas as pl
from jax.experimental.pallas import tpu as pltpu
from jax.sharding import PartitionSpec as P


data_step = 0.8
primal_step = 0.5
low_taps = (0.0625, 0.25, 0.375, 0.25, 0.0625)
high_taps = (-0.1, -0.3, 0.7, -0.2, -0.1)
low_reverse = (0.0625, 0.25, 0.375, 0.25, 0.0625)
high_reverse = (-0.1, -0.2, 0.7, -0.3, -0.1)

VMEM_LIMIT = 60 * 1024 * 1024


def c_add(x, y):
    if x[1] is None and y[1] is None:
        return (x[0] + y[0], None)
    if x[1] is None:
        return (x[0] + y[0], y[1])
    if y[1] is None:
        return (x[0] + y[0], x[1])
    return (x[0] + y[0], x[1] + y[1])


def c_sub(x, y):
    if x[1] is None and y[1] is None:
        return (x[0] - y[0], None)
    if x[1] is None:
        return (x[0] - y[0], -y[1])
    if y[1] is None:
        return (x[0] - y[0], x[1])
    return (x[0] - y[0], x[1] - y[1])


def c_rot(x, turn):
    turn = turn % 1.0
    wr, wi = math.cos(2 * math.pi * turn), math.sin(2 * math.pi * turn)
    re, im = x
    if turn == 0.0:
        return x
    if turn == 0.5:
        return (-re, None if im is None else -im)
    if turn == 0.25:
        return (jnp.zeros_like(re) if im is None else -im, re)
    if turn == 0.75:
        return (jnp.zeros_like(re) if im is None else im, -re)
    if im is None:
        return (re * wr, re * wi)
    if abs(abs(wr) - abs(wi)) < 1e-12:
        h = abs(wr)
        p, m = (re + im) * h, (re - im) * h
        if wr > 0:
            return (m, p) if wi > 0 else (p, -m)
        return (-p, m) if wi > 0 else (-m, -p)
    return (re * wr - im * wi, re * wi + im * wr)


def c_rot90_add(x, y, sign):
    re, im = x
    yr, yi = y
    if yi is not None:
        re = re - yi if sign > 0 else re + yi
    if im is None:
        im = yr if sign > 0 else -yr
    else:
        im = im + yr if sign > 0 else im - yr
    return (re, im)


def small_dft(xs, sign):
    n = len(xs)
    if n == 1:
        return list(xs)
    if n == 2:
        return [c_add(xs[0], xs[1]), c_sub(xs[0], xs[1])]
    if n % 4 == 0:
        parts = [small_dft(xs[r::4], sign) for r in range(4)]
        out = [None] * n
        for k in range(n // 4):
            t = [c_rot(parts[r][k], sign * r * k / n) for r in range(4)]
            s0, s1 = c_add(t[0], t[2]), c_sub(t[0], t[2])
            s2, s3 = c_add(t[1], t[3]), c_sub(t[1], t[3])
            out[k] = c_add(s0, s2)
            out[k + n // 2] = c_sub(s0, s2)
            out[k + n // 4] = c_rot90_add(s1, s3, sign)
            out[k + 3 * n // 4] = c_rot90_add(s1, s3, -sign)
        return out
    even, odd = small_dft(xs[0::2], sign), small_dft(xs[1::2], sign)
    out = [None] * n
    for k in range(n // 2):
        t = c_rot(odd[k], sign * k / n)
        out[k], out[k + n // 2] = c_add(even[k], t), c_sub(even[k], t)
    return out


def split_constant(table):
    high = table.astype(ml_dtypes.bfloat16)
    low = (table - high.astype(np.float64)).astype(ml_dtypes.bfloat16)
    return high, low


def dft_matrix(rows, cols, length, sign):
    angle = 2.0 * np.pi * ((np.asarray(rows)[:, None] * np.asarray(cols)[None, :]) % length) / length
    return np.cos(angle), sign * np.sin(angle)


def phase_rows(count, positions, length, sign):
    re, im = dft_matrix(np.arange(count), positions, length, sign)
    wide = lambda t: np.ascontiguousarray(np.broadcast_to(t[:, None, :], (count, 8, t.shape[1]))).astype(np.float32)
    return wide(re), wide(im)


def split_value(value):
    high = value.astype(jnp.bfloat16)
    low = (value - high.astype(jnp.float32)).astype(jnp.bfloat16)
    return high, low


def dot_nt(a, b):
    return lax.dot_general(a, b, (((1,), (1,)), ((), ())), preferred_element_type=jnp.float32)


def dot_split(high, low, value):
    v_high, v_low = split_value(value)
    return dot_nt(high, v_high) + (dot_nt(low, v_high) + dot_nt(high, v_low))


def lane_step(width):
    return 128 if width % 128 == 0 else width


def radix_stage(load, tw_re, tw_im, store, rows, width, count, sign):
    step = lane_step(width)

    def body(i, carry):
        at = pl.ds(pl.multiple_of(i * 8, 8), 8)
        for lane in range(0, width, step):
            lanes = slice(lane, lane + step)
            ys = small_dft([load(p, at, lanes) for p in range(count)], sign)
            for p in range(count):
                re, im = ys[p]
                if p == 0:
                    store(p, at, lanes, re, jnp.zeros_like(re) if im is None else im)
                    continue
                wr, wi = tw_re[p, :, lanes], tw_im[p, :, lanes]
                if im is None:
                    store(p, at, lanes, re * wr, re * wi)
                else:
                    store(p, at, lanes, re * wr - im * wi, re * wi + im * wr)
        return carry

    lax.fori_loop(0, rows // 8, body, 0)


def lane_tiles(width):
    step = lane_step(width)
    return width // step, step


def store_rows(out, lead, p, n, count, value):
    tiles, step = lane_tiles(value.shape[1])
    room = out.shape[-1]
    for t in range(tiles):
        piece = value[:, t * step : (t + 1) * step]
        if room > step:
            piece = jnp.concatenate([piece, jnp.zeros((n, room - step), piece.dtype)], axis=1)
        at = pl.ds(p, n, stride=count) if n > 1 else pl.ds(p, 1)
        out[(*lead, t, at, slice(None))] = piece


def mix_pair(f_high, f_low, y_re, y_im, half):
    a = dot_split(f_high[...], f_low[...], y_re)
    b = dot_split(f_high[...], f_low[...], y_im)
    return a[:half] - b[half:], b[:half] + a[half:]


def first_kernel(count, width, kept, x, tw_re, tw_im, f_high, f_low, out, y_re, y_im):
    rows = x.shape[0]

    def load(p, at, lanes):
        return (x[at, p * width + lanes.start : p * width + lanes.stop], None)

    def store(p, at, lanes, re, im):
        y_re[p, at, lanes] = re
        y_im[p, at, lanes] = im

    radix_stage(load, tw_re, tw_im, store, rows, width, count, -1)

    def body(p, carry):
        z_re, z_im = mix_pair(f_high, f_low, y_re[p], y_im[p], count * kept)
        for m in range(count):
            store_rows(out, (m, 0), p, kept, count, z_re[m * kept : (m + 1) * kept])
            store_rows(out, (m, 1), p, kept, count, z_im[m * kept : (m + 1) * kept])
        return carry

    lax.fori_loop(0, count, body, 0)


def flipped(ref, at, n):
    return jnp.concatenate([ref[t, at, :].T for t in range(ref.shape[0])], axis=0)[:n]


def middle_kernel(
    count, width, rows, got, dual, vis, weights, before, tw_re, tw_im, f_high, f_low, tv_re, tv_im, g_high, g_low,
    resid, out, sums, y_re, y_im, zt_re, zt_im, s_re, s_im,
):
    batch = got.shape[3]
    length = count * width
    per = width // count

    def load(p, at, lanes):
        tile = lanes.start // got.shape[4]
        return (got[p, 0, tile, at, :], got[p, 1, tile, at, :])

    def store(p, at, lanes, re, im):
        y_re[p, at, lanes] = re
        y_im[p, at, lanes] = im

    radix_stage(load, tw_re, tw_im, store, batch, width, count, -1)

    def forward(p, carry):
        z_re, z_im = mix_pair(f_high, f_low, y_re[p], y_im[p], width)
        store_rows(zt_re, (), p, width, count, z_re)
        store_rows(zt_im, (), p, width, count, z_im)
        return carry

    lax.fori_loop(0, count, forward, 0)

    def residual(i, carry):
        d_sum, v_sum = carry
        start = pl.multiple_of(i * 128, 128)
        at = pl.ds(start, 128)
        w = weights[0, :, at]
        v_re, v_im = vis[0, 0, :, at], vis[1, 0, :, at]
        d_re = dual[0, 0, :, at] * (1.0 / data_step) + w * flipped(zt_re, at, batch) - v_re
        d_im = dual[1, 0, :, at] * (1.0 / data_step) + w * flipped(zt_im, at, batch) - v_im
        resid[0, 0, :, at] = d_re
        resid[1, 0, :, at] = d_im
        s_re[:, at] = w * d_re
        s_im[:, at] = w * d_im
        fold = lambda t: jnp.sum(t.reshape(batch // 8, 8, 128), axis=0)
        return d_sum + fold(d_re * d_re + d_im * d_im), v_sum + fold(v_re * v_re + v_im * v_im)

    d_sum, v_sum = lax.fori_loop(0, length // 128, residual, (before[0], before[1]))
    sums[0] = d_sum
    sums[1] = v_sum
    if out.shape[3] > rows:
        step = out.shape[4]
        for m in range(count):
            for i, total in enumerate((d_sum, v_sum)):
                out[m, i, 0, rows:, :] = sum(total[:, at : at + step] for at in range(0, 128, step))

    def load_2(p, at, lanes):
        lanes = slice(p * width + lanes.start, p * width + lanes.stop)
        return (s_re[at, lanes], s_im[at, lanes])

    radix_stage(load_2, tv_re, tv_im, store, batch, width, count, 1)

    def inverse(p, carry):
        u_re, u_im = mix_pair(g_high, g_low, y_re[p], y_im[p], width)
        for m in range(count):
            store_rows(out, (m, 0), p, per, count, u_re[m * per : (m + 1) * per])
            store_rows(out, (m, 1), p, per, count, u_im[m * per : (m + 1) * per])
        return carry

    lax.fori_loop(0, count, inverse, 0)


def part_kernel(count, got, tw_re, tw_im, e_high, e_low, out, y_re, y_im):
    rows, batch = got.shape[3], got.shape[2] * got.shape[4]

    def load(p, at, lanes):
        tile = lanes.start // got.shape[4]
        return (got[p, 0, tile, at, :], got[p, 1, tile, at, :])

    def store(p, at, lanes, re, im):
        y_re[p, at, lanes] = re
        y_im[p, at, lanes] = im

    radix_stage(load, tw_re, tw_im, store, rows, batch, count, 1)

    def inverse(p, carry):
        out[p] = dot_split(e_high[...], e_low[...], jnp.concatenate([y_re[p], y_im[p]], axis=1))
        return carry

    lax.fori_loop(0, count, inverse, 0)


def last_kernel(count, width, rows, chunks, *refs):
    refs = list(refs)
    take = lambda n: [refs.pop(0) for _ in range(n)]
    (got_hbm,) = take(1)
    parts_hbm = take(chunks - 1)
    sky_hbm, own_hbm, other_hbm = take(3)
    resid_hbm = take(chunks)
    tw_re, tw_im, e_high, e_low, radius = take(5)
    out, fourier_hbm = take(2)
    got, part, sky, adjoint, resid, y_re, y_im, gt, sem = take(9)
    batch = got.shape[2] * got.shape[4]
    length = count * width
    half = rows // 2
    me = lax.axis_index("chan")
    copies = []

    def fetch(source, target):
        copy = pltpu.make_async_copy(source, target, sem.at[len(copies)])
        copies.append(copy)
        copy.start()
        return copy

    fetch_got = fetch(got_hbm, got)
    fetch_resid = [fetch(resid_hbm[c].at[:, 0], resid.at[c]) for c in range(chunks)]
    fetch_part = [fetch(p, part.at[i]) for i, p in enumerate(parts_hbm)]
    fetch_rest = [
        fetch(sky_hbm, sky),
        fetch(own_hbm, adjoint.at[pl.ds(pl.multiple_of(half * me, 8), half)]),
        fetch(other_hbm, adjoint.at[pl.ds(pl.multiple_of(half * (1 - me), 8), half)]),
    ]
    fetch_got.wait()
    totals = []
    for i in range(2):
        total = got[0, i, 0, rows:, :]
        for m in range(1, count):
            total = total + got[m, i, 0, rows:, :]
        totals.append(jnp.sum(total, keepdims=True))
    resid_norm, data_norm = totals
    shrink = data_step * (1.0 - radius[0] * jnp.sqrt(data_norm) / jnp.sqrt(resid_norm))

    def load(p, at, lanes):
        tile = lanes.start // got.shape[4]
        return (got[p, 0, tile, at, :], got[p, 1, tile, at, :])

    def store(p, at, lanes, re, im):
        y_re[p, at, lanes] = re
        y_im[p, at, lanes] = im

    radix_stage(load, tw_re, tw_im, store, rows, batch, count, 1)

    stores = []
    for c in range(chunks):
        fetch_resid[c].wait()
        per_chunk = resid.shape[2]
        for i in range(2):

            def scaled(j, carry, c=c, i=i):
                at = pl.ds(pl.multiple_of(j * 8, 8), 8)
                resid[c, i, at, :] = resid[c, i, at, :] * shrink
                return carry

            lax.fori_loop(0, per_chunk // 8, scaled, 0)
            copy = pltpu.make_async_copy(
                resid.at[c, i], fourier_hbm.at[i, 0, pl.ds(c * per_chunk, per_chunk)], sem.at[len(copies) + len(stores)]
            )
            copy.start()
            stores.append(copy)
    for copy in fetch_part:
        copy.wait()

    def inverse(p, carry):
        u = dot_split(e_high[...], e_low[...], jnp.concatenate([y_re[p], y_im[p]], axis=1))
        for i in range(chunks - 1):
            u = u + part[i, p]
        store_rows(gt, (), p, width, count, u)
        return carry

    lax.fori_loop(0, count, inverse, 0)
    for copy in fetch_rest:
        copy.wait()
    scale = primal_step * shrink

    def finish(i, carry):
        at = pl.ds(pl.multiple_of(i * 128, 128), 128)
        value = sky[:, at] - (scale * flipped(gt, at, rows) + primal_step * adjoint[:, at])
        out[:, at] = jnp.maximum(value, 0.0)
        return carry

    lax.fori_loop(0, length // 128, finish, 0)
    for copy in stores:
        copy.wait()


def vmem(shape, dtype=jnp.float32):
    return pltpu.VMEM(shape, dtype)


def whole(shape):
    return pl.BlockSpec(shape, lambda *_: (0,) * len(shape), pipeline_mode=pl.Buffered(1))


def call(kernel, args, specs, out_shape, out_specs, scratch, flops, moved):
    return pl.pallas_call(
        kernel,
        grid=(1,),
        in_specs=specs,
        out_specs=out_specs,
        out_shape=out_shape,
        scratch_shapes=scratch,
        cost_estimate=pl.CostEstimate(flops=flops, bytes_accessed=moved, transcendentals=0),
        compiler_params=pltpu.CompilerParams(vmem_limit_bytes=VMEM_LIMIT),
    )(*args)


def wave_kernel(
    count, sky, other, edge_own, edge_other, dual, above, below, limit,
    wave, own_out, other_out, x, w, sem,
):
    me = lax.axis_index("chan")
    row = lax.axis_index("row")
    half, width = limit.shape
    base = pl.multiple_of(8 * (1 - me), 8)
    copies = [
        pltpu.make_async_copy(
            sky.at[pl.ds(pl.multiple_of((half - 8) * me, 8), half + 8)], x.at[0, pl.ds(base, half + 8)], sem.at[0]
        ),
        pltpu.make_async_copy(other, x.at[1, pl.ds(base, half + 8)], sem.at[1]),
    ]
    edge = pl.ds(pl.multiple_of((half + 8) * me, 8), 8)
    copies.append(pltpu.make_async_copy(edge_own, x.at[0, edge], sem.at[2]))
    copies.append(pltpu.make_async_copy(edge_other, x.at[1, edge], sem.at[3]))
    for copy in copies:
        copy.start()
    for copy in copies:
        copy.wait()

    def analysis(source, start, n, low, high):
        if isinstance(start, int):
            taps = [source[start + p : start + p + n, :] for p in range(5)]
        else:
            window = source[pl.ds(pl.multiple_of(start - 6, 8), n + 16), :]
            taps = [window[6 + p : 6 + p + n] for p in range(5)]
        a = sum(high[p] * taps[p] for p in range(1, 5)) + high[0] * taps[0]
        b = sum(low[p] * taps[p] for p in range(1, 5)) + low[0] * taps[0]
        total = low[2] * a + high[2] * b
        pad = jnp.zeros((n, 128), jnp.float32)
        for p in (0, 1, 3, 4):
            mixed = jnp.concatenate([low[p] * a + high[p] * b, pad], axis=1)
            total = total + pltpu.roll(mixed, (2 - p) % (width + 128), 1)[:, :width]
        return total

    def shrunk(start, n, dual_own, dual_other, bound):
        s_own = dual_own + analysis(x.at[0], start - 2, n, low_taps, high_taps)
        s_other = dual_other + analysis(x.at[1], start - 2, n, low_taps, high_taps)
        factor = bound / jnp.maximum(jnp.sqrt(s_own * s_own + s_other * s_other), bound)
        return s_own * factor, s_other * factor

    first = jnp.logical_and(row == 0, me == 0)
    last = jnp.logical_and(row == count - 1, me == 1)
    for ref, start, out_side in ((above, 6, first), (below, half + 8, last)):
        a, b = shrunk(start, 2, ref[me], ref[1 - me], ref[2])
        w[0, pl.ds(start, 2), :] = jnp.where(out_side, 0.0, a)
        w[1, pl.ds(start, 2), :] = jnp.where(out_side, 0.0, b)

    def body(i, carry):
        at = pl.ds(pl.multiple_of(i * 8, 8), 8)
        a, b = shrunk(i * 8 + 8, 8, dual[me, at, :], dual[1 - me, at, :], limit[at, :])
        wave[me, at, :] = a
        wave[1 - me, at, :] = b
        inner = pl.ds(pl.multiple_of(i * 8 + 8, 8), 8)
        w[0, inner, :] = a
        w[1, inner, :] = b
        return carry

    lax.fori_loop(0, half // 8, body, 0)

    def back(i, carry):
        at = pl.ds(pl.multiple_of(i * 8, 8), 8)
        own_out[at, :] = analysis(w.at[0], i * 8 + 6, 8, low_reverse, high_reverse)
        other_out[at, :] = analysis(w.at[1], i * 8 + 6, 8, low_reverse, high_reverse)
        return carry

    lax.fori_loop(0, half // 8, back, 0)


def chan_swap(value):
    size = lax.axis_size("chan")
    return lax.ppermute(value, "chan", [(i, (i + 1) % size) for i in range(size)])


def edges_of(sky):
    count, size = lax.axis_size("row"), lax.axis_size("chan")
    top, bottom = sky[:8], sky[-8:]
    me = lax.axis_index("chan")
    at = lambda r, c: r * size + c
    own = [(at(r, 0), at(r + 1, 0)) for r in range(count - 1)] + [(at(r + 1, 1), at(r, 1)) for r in range(count - 1)]
    cross = [(at(r, 1), at(r + 1, 0)) for r in range(count - 1)] + [(at(r + 1, 0), at(r, 1)) for r in range(count - 1)]
    sent_own = jnp.where(me == 0, bottom, top)
    sent_cross = jnp.where(me == 0, top, bottom)
    axes = ("row", "chan")
    return lax.ppermute(sent_own, axes, own), lax.ppermute(sent_cross, axes, cross)


def facet_neighbours(wavelet_dual, reweight):
    axes = ("row", "chan")
    count = lax.axis_size(axes)
    up = [(i, i + 1) for i in range(count - 1)]
    down = [(j, i) for i, j in up]
    last = jnp.concatenate([wavelet_dual[:, -2:], reweight[None, -2:]])
    first = jnp.concatenate([wavelet_dual[:, :2], reweight[None, :2]])
    return lax.ppermute(last, axes, up), lax.ppermute(first, axes, down)


def per_device(sky_image, fourier_dual, visibilities, weights, radius, wavelet_dual, reweight):
    f32 = jnp.float32
    sky = sky_image[0]
    rows, length = sky.shape
    count = lax.axis_size("row")
    width = length // count
    per = width // count
    chunks = 2 if per % 2 == 0 else 1
    batch = width // chunks
    kept = per // chunks
    scale = 1.0 / math.sqrt(length)
    shape = jax.ShapeDtypeStruct

    def tile(high, wide):
        tiles, step = lane_tiles(wide)
        return tiles, high, step

    lanes = np.arange(width)
    tw = phase_rows(count, lanes, length, -1)
    tv = phase_rows(count, lanes, length, 1)
    f_table = split_constant(scale * np.concatenate(dft_matrix(lanes, lanes, width, -1)))
    g_table = split_constant(scale * np.concatenate(dft_matrix(lanes, lanes, width, 1)))

    sent = []
    for c in range(chunks):
        picked = (np.arange(count)[:, None] * per + c * kept + np.arange(kept)[None, :]).reshape(-1)
        table = split_constant(scale * np.concatenate(dft_matrix(picked, lanes, width, -1)))
        args = (sky, *tw, *table)
        piece = call(
            partial(first_kernel, count, width, kept), args, [whole(a.shape) for a in args],
            shape((count, 2, *tile(batch, rows)), f32), whole((count, 2, *tile(batch, rows))),
            [vmem((count, rows, width))] * 2, 10**10, 10**7,
        )
        sent.append(lax.all_to_all(piece, "row", split_axis=0, concat_axis=0, tiled=True))

    half = rows // 2
    me = lax.axis_index("chan")
    theirs = lax.dynamic_slice_in_dim(sky, (1 - me) * (half - 8), half + 8, 0)
    other = chan_swap(theirs)
    edge_own, edge_other = edges_of(sky)
    above, below = facet_neighbours(wavelet_dual, reweight)
    any_space = pl.BlockSpec(memory_space=pl.ANY)
    args = (sky, other, edge_own, edge_other, wavelet_dual, above, below, reweight)
    outs = (shape((2, half, length), f32), shape((half, length), f32), shape((half, length), f32))
    wavelet_new, adjoint_own, adjoint_other = call(
        partial(wave_kernel, count), args, [any_space] * 4 + [whole(a.shape) for a in args[4:]],
        outs, tuple(whole(o.shape) for o in outs),
        [vmem((2, half + 16, length))] * 2 + [pltpu.SemaphoreType.DMA((4,))], 10**10, 3 * 10**7,
    )
    adjoint_got = chan_swap(adjoint_other)

    resid, returned, sums = [], [], np.zeros((2, 8, 128), np.float32)
    for c in range(chunks):
        block = lambda lead, c=c: pl.BlockSpec(
            (*lead, batch, length), lambda i: (0,) * len(lead) + (c, 0), pipeline_mode=pl.Buffered(1)
        )
        tables = (*tw, *f_table, *tv, *g_table)
        outs = (
            shape((2, 1, batch, length), f32),
            shape((count, 2, *tile(rows + (8 if c == chunks - 1 else 0), batch)), f32),
            shape((2, 8, 128), f32),
        )
        d, piece, part = call(
            partial(middle_kernel, count, width, rows),
            (sent[c], fourier_dual, visibilities, weights, sums, *tables),
            [whole(sent[c].shape), block((2, 1)), block((2, 1)), block((1,)), *(whole(t.shape) for t in (sums, *tables))],
            outs, tuple(whole(o.shape) for o in outs),
            [vmem((count, batch, width))] * 2 + [vmem((-(-batch // 128), length, 128))] * 2 + [vmem((batch, length))] * 2,
            2 * 10**10, 3 * 10**7,
        )
        resid.append(d)
        sums = part
        returned.append(lax.all_to_all(piece, "row", split_axis=0, concat_axis=0, tiled=True))

    parts = []
    for c in range(chunks):
        q = c * batch + np.arange(batch)
        phases = phase_rows(count, q, length, 1)
        e_re, e_im = dft_matrix(lanes, q, width, 1)
        table = split_constant(scale * np.concatenate([e_re, -e_im], axis=1))
        scratch = [vmem((count, rows, batch))] * 2
        if c < chunks - 1:
            args = (returned[c], *phases, *table)
            out = shape((count, width, rows), f32)
            parts.append(
                call(
                    partial(part_kernel, count), args, [whole(a.shape) for a in args],
                    out, whole(out.shape), scratch, 10**10, 10**7,
                )
            )
            continue
        args = (returned[c], *parts, sky, adjoint_own, adjoint_got, *resid, *phases, *table, radius)
        specs = [any_space] * (4 + len(parts) + len(resid)) + [whole(a.shape) for a in (*phases, *table)]
        specs.append(pl.BlockSpec(memory_space=pltpu.SMEM))
        outs = (shape((rows, length), f32), shape((2, 1, width, length), f32))
        scratch = [
            vmem(returned[c].shape), vmem((max(1, chunks - 1), count, width, rows)), vmem((rows, length)),
            vmem((rows, length)), vmem((chunks, 2, batch, length)), *scratch,
            vmem((-(-rows // 128), length, 128)), pltpu.SemaphoreType.DMA((4 * chunks + 3,)),
        ]
        image_new, fourier_new = call(
            partial(last_kernel, count, width, rows, chunks), args, specs,
            outs, (whole(outs[0].shape), any_space), scratch, 10**10, 3 * 10**7,
        )
    return (image_new[None], fourier_new, wavelet_new)


def solution(mesh):
    in_specs = (
        P("chan", "row", None),
        P(None, "chan", "row", None),
        P(None, "chan", "row", None),
        P("chan", "row", None),
        P("chan"),
        P(None, ("row", "chan"), None),
        P(("row", "chan"), None),
    )
    out_specs = (
        P("chan", "row", None),
        P(None, "chan", "row", None),
        P(None, ("row", "chan"), None),
    )

    return jax.shard_map(per_device, mesh=mesh, in_specs=in_specs, out_specs=out_specs, check_vma=False)
```

```python
import math
from functools import partial

import jax
import jax.numpy as jnp
import ml_dtypes
import numpy as np
from jax import lax
from jax.experimental import pallas as pl
from jax.experimental.pallas import tpu as pltpu
from jax.sharding import PartitionSpec as P


data_step = 0.8
primal_step = 0.5
low_taps = (0.0625, 0.25, 0.375, 0.25, 0.0625)
high_taps = (-0.1, -0.3, 0.7, -0.2, -0.1)
low_reverse = (0.0625, 0.25, 0.375, 0.25, 0.0625)
high_reverse = (-0.1, -0.2, 0.7, -0.3, -0.1)

VMEM_LIMIT = 60 * 1024 * 1024


def c_add(x, y):
    if x[1] is None and y[1] is None:
        return (x[0] + y[0], None)
    if x[1] is None:
        return (x[0] + y[0], y[1])
    if y[1] is None:
        return (x[0] + y[0], x[1])
    return (x[0] + y[0], x[1] + y[1])


def c_sub(x, y):
    if x[1] is None and y[1] is None:
        return (x[0] - y[0], None)
    if x[1] is None:
        return (x[0] - y[0], -y[1])
    if y[1] is None:
        return (x[0] - y[0], x[1])
    return (x[0] - y[0], x[1] - y[1])


def c_rot(x, turn):
    turn = turn % 1.0
    wr, wi = math.cos(2 * math.pi * turn), math.sin(2 * math.pi * turn)
    re, im = x
    if turn == 0.0:
        return x
    if turn == 0.5:
        return (-re, None if im is None else -im)
    if turn == 0.25:
        return (jnp.zeros_like(re) if im is None else -im, re)
    if turn == 0.75:
        return (jnp.zeros_like(re) if im is None else im, -re)
    if im is None:
        return (re * wr, re * wi)
    if abs(abs(wr) - abs(wi)) < 1e-12:
        h = abs(wr)
        p, m = (re + im) * h, (re - im) * h
        if wr > 0:
            return (m, p) if wi > 0 else (p, -m)
        return (-p, m) if wi > 0 else (-m, -p)
    return (re * wr - im * wi, re * wi + im * wr)


def c_rot90_add(x, y, sign):
    re, im = x
    yr, yi = y
    if yi is not None:
        re = re - yi if sign > 0 else re + yi
    if im is None:
        im = yr if sign > 0 else -yr
    else:
        im = im + yr if sign > 0 else im - yr
    return (re, im)


def small_dft(xs, sign):
    n = len(xs)
    if n == 1:
        return list(xs)
    if n == 2:
        return [c_add(xs[0], xs[1]), c_sub(xs[0], xs[1])]
    if n % 4 == 0:
        parts = [small_dft(xs[r::4], sign) for r in range(4)]
        out = [None] * n
        for k in range(n // 4):
            t = [c_rot(parts[r][k], sign * r * k / n) for r in range(4)]
            s0, s1 = c_add(t[0], t[2]), c_sub(t[0], t[2])
            s2, s3 = c_add(t[1], t[3]), c_sub(t[1], t[3])
            out[k] = c_add(s0, s2)
            out[k + n // 2] = c_sub(s0, s2)
            out[k + n // 4] = c_rot90_add(s1, s3, sign)
            out[k + 3 * n // 4] = c_rot90_add(s1, s3, -sign)
        return out
    even, odd = small_dft(xs[0::2], sign), small_dft(xs[1::2], sign)
    out = [None] * n
    for k in range(n // 2):
        t = c_rot(odd[k], sign * k / n)
        out[k], out[k + n // 2] = c_add(even[k], t), c_sub(even[k], t)
    return out


def split_constant(table):
    high = table.astype(ml_dtypes.bfloat16)
    low = (table - high.astype(np.float64)).astype(ml_dtypes.bfloat16)
    return high, low


def dft_matrix(rows, cols, length, sign):
    angle = 2.0 * np.pi * ((np.asarray(rows)[:, None] * np.asarray(cols)[None, :]) % length) / length
    return np.cos(angle), sign * np.sin(angle)


def phase_rows(count, positions, length):
    wide = lambda t: np.ascontiguousarray(np.broadcast_to(t[:, None, :], (count, 8, t.shape[1]))).astype(np.float32)
    re, im = dft_matrix(np.arange(count), positions, length, 1)
    return wide(re), wide(im)


def split_value(value):
    high = value.astype(jnp.bfloat16)
    low = (value - high.astype(jnp.float32)).astype(jnp.bfloat16)
    return high, low


def dot_nt(a, b):
    return lax.dot_general(a, b, (((1,), (1,)), ((), ())), preferred_element_type=jnp.float32)


def dot_split(high, low, value):
    v_high, v_low = split_value(value)
    return dot_nt(high, v_high) + (dot_nt(low, v_high) + dot_nt(high, v_low))


def lane_step(width):
    return 128 if width % 128 == 0 else width


def radix_stage(load, tw_re, tw_im, store, rows, width, count, sign, shift=0):
    step = lane_step(width)
    low, high = rows if isinstance(rows, tuple) else (0, rows)

    def body(i, carry):
        at = pl.ds(pl.multiple_of(i * 8, 8), 8)
        for lane in range(0, width, step):
            lanes = slice(lane, lane + step)
            ys = small_dft([load(p, at, lanes) for p in range(count)], sign)
            for p in range(count):
                re, im = ys[p]
                if p == 0:
                    store(p, at, lanes, re, jnp.zeros_like(re) if im is None else im)
                    continue
                from_table = slice(shift + lane, shift + lane + step)
                wr, wi = tw_re[p, :, from_table], tw_im[p, :, from_table]
                if im is None:
                    store(p, at, lanes, re * wr, re * wi if sign > 0 else -(re * wi))
                elif sign > 0:
                    store(p, at, lanes, re * wr - im * wi, re * wi + im * wr)
                else:
                    store(p, at, lanes, re * wr + im * wi, im * wr - re * wi)
        return carry

    lax.fori_loop(low // 8, high // 8, body, 0)


def lane_tiles(width):
    step = lane_step(width)
    return width // step, step


def store_rows(out, lead, p, n, count, value):
    tiles, step = lane_tiles(value.shape[1])
    room = out.shape[-1]
    for t in range(tiles):
        piece = value[:, t * step : (t + 1) * step]
        if room > step:
            piece = jnp.concatenate([piece, jnp.zeros((n, room - step), piece.dtype)], axis=1)
        at = pl.ds(p, n, stride=count) if n > 1 else pl.ds(p, 1)
        out[(*lead, t, at, slice(None))] = piece


def mix_pair(g_high, g_low, y_re, y_im, half, sign):
    a = dot_split(g_high[...], g_low[...], y_re)
    b = dot_split(g_high[...], g_low[...], y_im)
    if sign > 0:
        return a[:half] - b[half:], b[:half] + a[half:]
    return a[:half] + b[half:], b[:half] - a[half:]


def fetch_pieces(pieces, target, sem):
    me = lax.axis_index("row")
    copies = []
    for d, piece in enumerate(pieces):
        place = target if len(pieces) == 1 else target.at[jnp.bitwise_xor(me, d)]
        copies.append(pltpu.make_async_copy(piece, place, sem.at[d]))
        copies[-1].start()
    return copies


def store_pieces(source, pieces, sem):
    me = lax.axis_index("row")
    copies = []
    for d, piece in enumerate(pieces):
        place = source if len(pieces) == 1 else source.at[jnp.bitwise_xor(me, d)]
        copies.append(pltpu.make_async_copy(place, piece, sem.at[d]))
        copies[-1].start()
    for copy in copies:
        copy.wait()


def first_kernel(count, width, kept, n, x_hbm, tw_re, tw_im, f_high, f_low, *refs):
    pieces, (x, out, y_re, y_im, x_sem, sem) = refs[:n], refs[n:]
    rows = x.shape[0]
    parts = SKY_PARTS if rows % (8 * SKY_PARTS) == 0 else 1
    copies = []
    for i in range(parts):
        at = pl.ds(i * (rows // parts), rows // parts)
        copies.append(pltpu.make_async_copy(x_hbm.at[at], x.at[at], x_sem.at[i]))
        copies[-1].start()

    def load(p, at, lanes):
        return (x[at, p * width + lanes.start : p * width + lanes.stop], None)

    def store(p, at, lanes, re, im):
        y_re[p, at, lanes] = re
        y_im[p, at, lanes] = im

    for i in range(parts):
        copies[i].wait()
        span = (i * (rows // parts), (i + 1) * (rows // parts))
        radix_stage(load, tw_re, tw_im, store, span, width, count, -1)

    def body(p, carry):
        z_re, z_im = mix_pair(f_high, f_low, y_re[p], y_im[p], count * kept, -1)
        for m in range(count):
            store_rows(out, (m, 0), p, kept, count, z_re[m * kept : (m + 1) * kept])
            store_rows(out, (m, 1), p, kept, count, z_im[m * kept : (m + 1) * kept])
        return carry

    lax.fori_loop(0, count, body, 0, unroll=UNROLL)
    store_pieces(out, pieces, sem)


def flipped(ref, at, n):
    return jnp.concatenate([ref[t, at, :].T for t in range(ref.shape[0])], axis=0)[:n]


def middle_kernel(count, width, n, *refs):
    came, refs = refs[:n], refs[n:]
    dual, vis, weights, before, tw_re, tw_im, g_high, g_low, resid, sums = refs[:10]
    pieces, refs = refs[10 : 10 + n], refs[10 + n :]
    got, out, y_re, y_im, zt_re, zt_im, s_re, s_im, sem = refs
    for copy in fetch_pieces(came, got, sem):
        copy.wait()
    batch = got.shape[3]
    length = count * width
    per = width // count

    def load(p, at, lanes):
        tile = lanes.start // got.shape[4]
        return (got[p, 0, tile, at, :], got[p, 1, tile, at, :])

    def store(p, at, lanes, re, im):
        y_re[p, at, lanes] = re
        y_im[p, at, lanes] = im

    radix_stage(load, tw_re, tw_im, store, batch, width, count, -1)

    def forward(p, carry):
        z_re, z_im = mix_pair(g_high, g_low, y_re[p], y_im[p], width, -1)
        store_rows(zt_re, (), p, width, count, z_re)
        store_rows(zt_im, (), p, width, count, z_im)
        return carry

    lax.fori_loop(0, count, forward, 0, unroll=UNROLL)

    def residual(i, carry):
        d_sum, v_sum = carry
        start = pl.multiple_of(i * 128, 128)
        at = pl.ds(start, 128)
        w = weights[0, :, at]
        v_re, v_im = vis[0, 0, :, at], vis[1, 0, :, at]
        d_re = dual[0, 0, :, at] * (1.0 / data_step) + w * flipped(zt_re, at, batch) - v_re
        d_im = dual[1, 0, :, at] * (1.0 / data_step) + w * flipped(zt_im, at, batch) - v_im
        resid[0, 0, :, at] = d_re
        resid[1, 0, :, at] = d_im
        s_re[:, at] = w * d_re
        s_im[:, at] = w * d_im
        fold = lambda t: jnp.sum(t.reshape(batch // 8, 8, 128), axis=0)
        return d_sum + fold(d_re * d_re + d_im * d_im), v_sum + fold(v_re * v_re + v_im * v_im)

    d_sum, v_sum = lax.fori_loop(0, length // 128, residual, (before[0], before[1]))
    sums[0] = d_sum
    sums[1] = v_sum

    def load_2(p, at, lanes):
        lanes = slice(p * width + lanes.start, p * width + lanes.stop)
        return (s_re[at, lanes], s_im[at, lanes])

    radix_stage(load_2, tw_re, tw_im, store, batch, width, count, 1)

    def inverse(p, carry):
        u_re, u_im = mix_pair(g_high, g_low, y_re[p], y_im[p], width, 1)
        for m in range(count):
            store_rows(out, (m, 0), p, per, count, u_re[m * per : (m + 1) * per])
            store_rows(out, (m, 1), p, per, count, u_im[m * per : (m + 1) * per])
        return carry

    lax.fori_loop(0, count, inverse, 0, unroll=UNROLL)
    store_pieces(out, pieces, sem)


def last_kernel(count, width, start, n, is_first, is_last, *refs):
    came, refs = refs[:n], list(refs[n:])
    take = lambda k: [refs.pop(0) for _ in range(k)]
    base_hbm = take(3 if is_first else 1)
    tw_re, tw_im, g_high, g_low, shrink, out_hbm, got, base, y_re, y_im, gt, sem, came_sem = take(13)
    adjoint = refs.pop(0) if is_first else None
    rows, batch = got.shape[3], got.shape[2] * got.shape[4]
    length = count * width
    me = lax.axis_index("chan")
    fetch_got = fetch_pieces(came, got, came_sem)
    half = rows // 2
    fetch_base = [pltpu.make_async_copy(base_hbm[0], base, sem.at[0])]
    if is_first:
        for i, side in enumerate((me, 1 - me)):
            place = adjoint.at[pl.ds(pl.multiple_of(half * side, 8), half)]
            fetch_base.append(pltpu.make_async_copy(base_hbm[1 + i], place, sem.at[1 + i]))
    for copy in fetch_base:
        copy.start()
    for copy in fetch_got:
        copy.wait()

    def load(p, at, lanes):
        tile = lanes.start // got.shape[4]
        return (got[p, 0, tile, at, :], got[p, 1, tile, at, :])

    def store(p, at, lanes, re, im):
        y_re[p, at, lanes] = re
        y_im[p, at, lanes] = im

    radix_stage(load, tw_re, tw_im, store, rows, batch, count, 1, start)
    cols = slice(start, start + batch)
    e_high = jnp.concatenate([g_high[:width, cols], -g_high[width:, cols]], axis=1)
    e_low = jnp.concatenate([g_low[:width, cols], -g_low[width:, cols]], axis=1)

    def inverse(p, carry):
        u = dot_split(e_high, e_low, jnp.concatenate([y_re[p], y_im[p]], axis=1))
        store_rows(gt, (), p, width, count, u)
        return carry

    lax.fori_loop(0, count, inverse, 0, unroll=UNROLL)
    for copy in fetch_base:
        copy.wait()
    scale = primal_step * shrink[0]
    groups = 4
    stores = []
    for g in range(groups):
        tiles = length // 128 // groups

        def finish(i, carry):
            at = pl.ds(pl.multiple_of(i * 128, 128), 128)
            value = base[:, at] - scale * flipped(gt, at, rows)
            if is_first:
                value = value - primal_step * adjoint[:, at]
            base[:, at] = jnp.maximum(value, 0.0) if is_last else value
            return carry

        lax.fori_loop(g * tiles, (g + 1) * tiles, finish, 0, unroll=UNROLL)
        at = pl.ds(g * tiles * 128, tiles * 128)
        stores.append(pltpu.make_async_copy(base.at[:, at], out_hbm.at[:, at], sem.at[3 + g]))
        stores[-1].start()
    for copy in stores:
        copy.wait()


def vmem(shape, dtype=jnp.float32):
    return pltpu.VMEM(shape, dtype)


def whole(shape):
    return pl.BlockSpec(shape, lambda *_: (0,) * len(shape), pipeline_mode=pl.Buffered(1))


def call(kernel, args, specs, out_shape, out_specs, scratch, flops, moved):
    return pl.pallas_call(
        kernel,
        grid=(1,),
        in_specs=specs,
        out_specs=out_specs,
        out_shape=out_shape,
        scratch_shapes=scratch,
        cost_estimate=pl.CostEstimate(flops=flops, bytes_accessed=moved, transcendentals=0),
        compiler_params=pltpu.CompilerParams(vmem_limit_bytes=VMEM_LIMIT),
    )(*args)


def analysis(source, start, n, low, high):
    if isinstance(start, int):
        taps = [source[start + p : start + p + n, :] for p in range(5)]
    else:
        window = source[pl.ds(pl.multiple_of(start - 6, 8), n + 16), :]
        taps = [window[6 + p : 6 + p + n] for p in range(5)]
    width = taps[0].shape[1]

    def along(coefs):
        if coefs[0] == coefs[4]:
            total = coefs[2] * taps[2] + coefs[0] * (taps[0] + taps[4])
        else:
            total = coefs[2] * taps[2] + (coefs[0] * taps[0] + coefs[4] * taps[4])
        if coefs[1] == coefs[3]:
            return total + coefs[1] * (taps[1] + taps[3])
        return total + (coefs[1] * taps[1] + coefs[3] * taps[3])

    a, b = along(high), along(low)
    total = low[2] * a + high[2] * b
    pad = jnp.zeros((n, 128), jnp.float32)
    mixed = {}
    for p in (0, 1, 3, 4):
        pair = (low[p], high[p])
        if pair not in mixed:
            mixed[pair] = jnp.concatenate([low[p] * a + high[p] * b, pad], axis=1)
        total = total + pltpu.roll(mixed[pair], (2 - p) % (width + 128), 1)[:, :width]
    return total


def wave_kernel(
    count, sky, other, edge_own, edge_other, dual, above, below, limit, wave, outside, x, sem
):
    me = lax.axis_index("chan")
    row = lax.axis_index("row")
    half = limit.shape[0]
    base = pl.multiple_of(8 * (1 - me), 8)
    edge = pl.ds(pl.multiple_of((half + 8) * me, 8), 8)
    own_rows = pl.ds(pl.multiple_of((half - 8) * me, 8), half + 8)
    copies = [
        pltpu.make_async_copy(sky.at[own_rows], x.at[0, pl.ds(base, half + 8)], sem.at[0]),
        pltpu.make_async_copy(other, x.at[1, pl.ds(base, half + 8)], sem.at[1]),
        pltpu.make_async_copy(edge_own, x.at[0, edge], sem.at[2]),
        pltpu.make_async_copy(edge_other, x.at[1, edge], sem.at[3]),
    ]
    for copy in copies:
        copy.start()
    for copy in copies:
        copy.wait()

    def shrunk(start, n, dual_own, dual_other, bound):
        s_own = dual_own + analysis(x.at[0], start - 2, n, low_taps, high_taps)
        s_other = dual_other + analysis(x.at[1], start - 2, n, low_taps, high_taps)
        factor = bound / jnp.maximum(jnp.sqrt(s_own * s_own + s_other * s_other), bound)
        return s_own * factor, s_other * factor

    first = jnp.logical_and(row == 0, me == 0)
    last = jnp.logical_and(row == count - 1, me == 1)
    outside[...] = jnp.zeros_like(outside)
    for side, (ref, start, beyond) in enumerate(((above, 6, first), (below, half + 8, last))):
        a, b = shrunk(start, 2, ref[me], ref[1 - me], ref[2])
        at = slice(6, 8) if side == 0 else slice(0, 2)
        outside[0, side, at, :] = jnp.where(beyond, 0.0, a)
        outside[1, side, at, :] = jnp.where(beyond, 0.0, b)

    def body(i, carry):
        at = pl.ds(pl.multiple_of(i * 8, 8), 8)
        a, b = shrunk(i * 8 + 8, 8, dual[me, at, :], dual[1 - me, at, :], limit[at, :])
        wave[me, at, :] = a
        wave[1 - me, at, :] = b
        return carry

    lax.fori_loop(0, half // 8, body, 0)


def adjoint_kernel(wave, outside, own_out, other_out, w, sem):
    me = lax.axis_index("chan")
    half = own_out.shape[0]
    copies = []
    for i, plane in enumerate((me, 1 - me)):
        copies.append(pltpu.make_async_copy(wave.at[plane], w.at[i, pl.ds(8, half)], sem.at[i, 0]))
        copies.append(pltpu.make_async_copy(outside.at[i, 0], w.at[i, pl.ds(0, 8)], sem.at[i, 1]))
        copies.append(pltpu.make_async_copy(outside.at[i, 1], w.at[i, pl.ds(half + 8, 8)], sem.at[i, 2]))
    for copy in copies:
        copy.start()
    for copy in copies:
        copy.wait()

    def back(i, carry):
        at = pl.ds(pl.multiple_of(i * 8, 8), 8)
        own_out[at, :] = analysis(w.at[0], i * 8 + 6, 8, low_reverse, high_reverse)
        other_out[at, :] = analysis(w.at[1], i * 8 + 6, 8, low_reverse, high_reverse)
        return carry

    lax.fori_loop(0, half // 8, back, 0)


def chan_swap(value):
    size = lax.axis_size("chan")
    return lax.ppermute(value, "chan", [(i, (i + 1) % size) for i in range(size)])


UNROLL = 2
SKY_PARTS = 4


def partners(size):
    quarter = size // 4
    far = [d for i in range(quarter) for d in (2 * quarter + i, 3 * quarter + i)]
    return far[:2] + [*range(quarter, 2 * quarter), *range(1, quarter)] + far[2:]


def row_exchange(pieces):
    if len(pieces) == 1:
        return [lax.all_to_all(pieces[0], "row", split_axis=0, concat_axis=0, tiled=True)]
    size = len(pieces)
    got = list(pieces)
    for d in reversed(partners(size)):
        got[d] = lax.ppermute(pieces[d], "row", [(i, i ^ d) for i in range(size)])
    return got


def row_total(value):
    size = lax.axis_size("row")
    away = lambda v, d: lax.ppermute(v, "row", [(i, i ^ d) for i in range(size)])
    value = value + away(value, 1)
    return value + sum(away(value, d) for d in range(2, size, 2))


def edges_of(sky):
    count, size = lax.axis_size("row"), lax.axis_size("chan")
    top, bottom = sky[:8], sky[-8:]
    me = lax.axis_index("chan")
    at = lambda r, c: r * size + c
    own = [(at(r, 0), at(r + 1, 0)) for r in range(count - 1)] + [(at(r + 1, 1), at(r, 1)) for r in range(count - 1)]
    cross = [(at(r, 1), at(r + 1, 0)) for r in range(count - 1)] + [(at(r + 1, 0), at(r, 1)) for r in range(count - 1)]
    sent_own = jnp.where(me == 0, bottom, top)
    sent_cross = jnp.where(me == 0, top, bottom)
    axes = ("row", "chan")
    return lax.ppermute(sent_own, axes, own), lax.ppermute(sent_cross, axes, cross)


def facet_neighbours(wavelet_dual, reweight):
    axes = ("row", "chan")
    count = lax.axis_size(axes)
    up = [(i, i + 1) for i in range(count - 1)]
    down = [(j, i) for i, j in up]
    last = jnp.concatenate([wavelet_dual[:, -2:], reweight[None, -2:]])
    first = jnp.concatenate([wavelet_dual[:, :2], reweight[None, :2]])
    return lax.ppermute(last, axes, up), lax.ppermute(first, axes, down)


def per_device(sky_image, fourier_dual, visibilities, weights, radius, wavelet_dual, reweight):
    f32 = jnp.float32
    sky = sky_image[0]
    rows, length = sky.shape
    count = lax.axis_size("row")
    width = length // count
    per = width // count
    chunks = 2 if per % 2 == 0 else 1
    batch = width // chunks
    kept = per // chunks
    scale = 1.0 / math.sqrt(length)
    shape = jax.ShapeDtypeStruct

    any_space = pl.BlockSpec(memory_space=pl.ANY)
    dma = lambda n: pltpu.SemaphoreType.DMA((n,))
    n = count if count & (count - 1) == 0 and count <= 16 else 1
    pieces_of = lambda packed: [shape(packed[1:], f32)] * n if n > 1 else [shape(packed, f32)]

    def tile(high, wide):
        tiles, step = lane_tiles(wide)
        return tiles, high, step

    lanes = np.arange(width)
    tw = phase_rows(count, lanes, length)
    g_table = split_constant(scale * np.concatenate(dft_matrix(lanes, lanes, width, 1)))

    sent = []
    for c in range(chunks):
        picked = (np.arange(count)[:, None] * per + c * kept + np.arange(kept)[None, :]).reshape(-1)
        table = split_constant(scale * np.concatenate(dft_matrix(picked, lanes, width, 1)))
        args = (sky, *tw, *table)
        packed = (count, 2, *tile(batch, rows))
        piece = call(
            partial(first_kernel, count, width, kept, n), args,
            [any_space] + [whole(a.shape) for a in args[1:]], pieces_of(packed), [any_space] * n,
            [vmem(sky.shape), vmem(packed)] + [vmem((count, rows, width))] * 2 + [dma(SKY_PARTS), dma(n)],
            10**10, 10**7,
        )
        sent.append(row_exchange(piece))

    half = rows // 2
    me = lax.axis_index("chan")
    theirs = lax.dynamic_slice_in_dim(sky, (1 - me) * (half - 8), half + 8, 0)
    other = chan_swap(theirs)
    edge_own, edge_other = edges_of(sky)
    above, below = facet_neighbours(wavelet_dual, reweight)
    args = (sky, other, edge_own, edge_other, wavelet_dual, above, below, reweight)
    outs = (shape((2, half, length), f32), shape((2, 2, 8, length), f32))
    wavelet_new, outside = call(
        partial(wave_kernel, count), args, [any_space] * 4 + [whole(a.shape) for a in args[4:]],
        outs, tuple(whole(o.shape) for o in outs),
        [vmem((2, half + 16, length)), dma(4)], 10**10, 3 * 10**7,
    )
    outs = (shape((half, length), f32), shape((half, length), f32))
    adjoint_own, adjoint_other = call(
        adjoint_kernel, (wavelet_new, outside), [any_space] * 2, outs, tuple(whole(o.shape) for o in outs),
        [vmem((2, half + 16, length)), pltpu.SemaphoreType.DMA((2, 3))], 10**10, 3 * 10**7,
    )
    adjoint_got = chan_swap(adjoint_other)

    resid, returned, sums = [], [], np.zeros((2, 8, 128), np.float32)
    for c in range(chunks):
        block = lambda lead, c=c: pl.BlockSpec(
            (*lead, batch, length), lambda i: (0,) * len(lead) + (c, 0), pipeline_mode=pl.Buffered(1)
        )
        tables = (*tw, *g_table)
        coming = (count, 2, *tile(batch, rows))
        packed = (count, 2, *tile(rows, batch))
        outs = (shape((2, 1, batch, length), f32), shape((2, 8, 128), f32))
        d, part, *piece = call(
            partial(middle_kernel, count, width, n),
            (*sent[c], fourier_dual, visibilities, weights, sums, *tables),
            [any_space] * n + [block((2, 1)), block((2, 1)), block((1,)), *(whole(t.shape) for t in (sums, *tables))],
            [*outs, *pieces_of(packed)], [whole(o.shape) for o in outs] + [any_space] * n,
            [vmem(coming), vmem(packed)] + [vmem((count, batch, width))] * 2 + [vmem((-(-batch // 128), length, 128))] * 2 + [vmem((batch, length))] * 2 + [dma(n)],
            2 * 10**10, 3 * 10**7,
        )
        resid.append(d)
        sums = part
        returned.append(row_exchange(piece))

    total = row_total(sums) if n > 1 else lax.psum(sums, "row")
    data_norm = jnp.sum(total[1])
    resid_norm = jnp.sum(total[0])
    shrink = data_step * (1.0 - radius * jnp.sqrt(data_norm) / jnp.sqrt(resid_norm))
    fourier_new = jnp.concatenate([d * shrink for d in resid], axis=2)

    base = (sky, adjoint_own, adjoint_got)
    for c in range(chunks):
        packed = (count, 2, *tile(rows, batch))
        args = (*returned[c], *base, *tw, *g_table, shrink)
        specs = [any_space] * (n + len(base)) + [whole(a.shape) for a in (*tw, *g_table)]
        specs.append(pl.BlockSpec(memory_space=pltpu.SMEM))
        scratch = [
            vmem(packed), vmem((rows, length)), *[vmem((count, rows, batch))] * 2,
            vmem((-(-rows // 128), length, 128)), dma(7), dma(n), *[vmem((rows, length))] * (c == 0),
        ]
        image_new = call(
            partial(last_kernel, count, width, c * batch, n, c == 0, c == chunks - 1), args, specs,
            shape((rows, length), f32), any_space, scratch, 10**10, 3 * 10**7,
        )
        base = (image_new,)
    return (image_new[None], fourier_new, wavelet_new)


def solution(mesh):
    in_specs = (
        P("chan", "row", None),
        P(None, "chan", "row", None),
        P(None, "chan", "row", None),
        P("chan", "row", None),
        P("chan"),
        P(None, ("row", "chan"), None),
        P(("row", "chan"), None),
    )
    out_specs = (
        P("chan", "row", None),
        P(None, "chan", "row", None),
        P(None, ("row", "chan"), None),
    )

    return jax.shard_map(per_device, mesh=mesh, in_specs=in_specs, out_specs=out_specs, check_vma=False)
```

```python
import math
from functools import partial

import jax
import jax.numpy as jnp
import ml_dtypes
import numpy as np
from jax import lax
from jax.experimental import pallas as pl
from jax.experimental.pallas import tpu as pltpu
from jax.sharding import PartitionSpec as P


data_step = 0.8
primal_step = 0.5
low_taps = (0.0625, 0.25, 0.375, 0.25, 0.0625)
high_taps = (-0.1, -0.3, 0.7, -0.2, -0.1)
low_reverse = (0.0625, 0.25, 0.375, 0.25, 0.0625)
high_reverse = (-0.1, -0.2, 0.7, -0.3, -0.1)

VMEM_LIMIT = 60 * 1024 * 1024


def c_add(x, y):
    if x[1] is None and y[1] is None:
        return (x[0] + y[0], None)
    if x[1] is None:
        return (x[0] + y[0], y[1])
    if y[1] is None:
        return (x[0] + y[0], x[1])
    return (x[0] + y[0], x[1] + y[1])


def c_sub(x, y):
    if x[1] is None and y[1] is None:
        return (x[0] - y[0], None)
    if x[1] is None:
        return (x[0] - y[0], -y[1])
    if y[1] is None:
        return (x[0] - y[0], x[1])
    return (x[0] - y[0], x[1] - y[1])


def c_rot(x, turn):
    turn = turn % 1.0
    wr, wi = math.cos(2 * math.pi * turn), math.sin(2 * math.pi * turn)
    re, im = x
    if turn == 0.0:
        return x
    if turn == 0.5:
        return (-re, None if im is None else -im)
    if turn == 0.25:
        return (jnp.zeros_like(re) if im is None else -im, re)
    if turn == 0.75:
        return (jnp.zeros_like(re) if im is None else im, -re)
    if im is None:
        return (re * wr, re * wi)
    if abs(abs(wr) - abs(wi)) < 1e-12:
        h = abs(wr)
        p, m = (re + im) * h, (re - im) * h
        if wr > 0:
            return (m, p) if wi > 0 else (p, -m)
        return (-p, m) if wi > 0 else (-m, -p)
    return (re * wr - im * wi, re * wi + im * wr)


def c_rot90_add(x, y, sign):
    re, im = x
    yr, yi = y
    if yi is not None:
        re = re - yi if sign > 0 else re + yi
    if im is None:
        im = yr if sign > 0 else -yr
    else:
        im = im + yr if sign > 0 else im - yr
    return (re, im)


def small_dft(xs, sign):
    n = len(xs)
    if n == 1:
        return list(xs)
    if n == 2:
        return [c_add(xs[0], xs[1]), c_sub(xs[0], xs[1])]
    if n % 4 == 0:
        parts = [small_dft(xs[r::4], sign) for r in range(4)]
        out = [None] * n
        for k in range(n // 4):
            t = [c_rot(parts[r][k], sign * r * k / n) for r in range(4)]
            s0, s1 = c_add(t[0], t[2]), c_sub(t[0], t[2])
            s2, s3 = c_add(t[1], t[3]), c_sub(t[1], t[3])
            out[k] = c_add(s0, s2)
            out[k + n // 2] = c_sub(s0, s2)
            out[k + n // 4] = c_rot90_add(s1, s3, sign)
            out[k + 3 * n // 4] = c_rot90_add(s1, s3, -sign)
        return out
    even, odd = small_dft(xs[0::2], sign), small_dft(xs[1::2], sign)
    out = [None] * n
    for k in range(n // 2):
        t = c_rot(odd[k], sign * k / n)
        out[k], out[k + n // 2] = c_add(even[k], t), c_sub(even[k], t)
    return out


def split_constant(table):
    high = table.astype(ml_dtypes.bfloat16)
    low = (table - high.astype(np.float64)).astype(ml_dtypes.bfloat16)
    return high, low


def dft_matrix(rows, cols, length, sign):
    angle = 2.0 * np.pi * ((np.asarray(rows)[:, None] * np.asarray(cols)[None, :]) % length) / length
    return np.cos(angle), sign * np.sin(angle)


def phase_rows(count, positions, length):
    wide = lambda t: np.ascontiguousarray(np.broadcast_to(t[:, None, :], (count, 8, t.shape[1]))).astype(np.float32)
    re, im = dft_matrix(np.arange(count), positions, length, 1)
    return wide(re), wide(im)


def split_value(value):
    high = value.astype(jnp.bfloat16)
    low = (value - high.astype(jnp.float32)).astype(jnp.bfloat16)
    return high, low


def dot_nt(a, b):
    return lax.dot_general(a, b, (((1,), (1,)), ((), ())), preferred_element_type=jnp.float32)


def dot_split(high, low, value):
    v_high, v_low = split_value(value)
    return dot_nt(high, v_high) + (dot_nt(low, v_high) + dot_nt(high, v_low))


def lane_step(width):
    return 128 if width % 128 == 0 else width


def radix_stage(load, tw_re, tw_im, store, rows, width, count, sign, shift=0):
    step = lane_step(width)
    low, high = rows if isinstance(rows, tuple) else (0, rows)

    def body(i, carry):
        at = pl.ds(pl.multiple_of(i * 8, 8), 8)
        for lane in range(0, width, step):
            lanes = slice(lane, lane + step)
            ys = small_dft([load(p, at, lanes) for p in range(count)], sign)
            for p in range(count):
                re, im = ys[p]
                if p == 0:
                    store(p, at, lanes, re, jnp.zeros_like(re) if im is None else im)
                    continue
                from_table = slice(shift + lane, shift + lane + step)
                wr, wi = tw_re[p, :, from_table], tw_im[p, :, from_table]
                if im is None:
                    store(p, at, lanes, re * wr, re * wi if sign > 0 else -(re * wi))
                elif sign > 0:
                    store(p, at, lanes, re * wr - im * wi, re * wi + im * wr)
                else:
                    store(p, at, lanes, re * wr + im * wi, im * wr - re * wi)
        return carry

    lax.fori_loop(low // 8, high // 8, body, 0, unroll=2)


def lane_tiles(width):
    step = lane_step(width)
    return width // step, step


def store_rows(out, lead, p, n, count, value):
    tiles, step = lane_tiles(value.shape[1])
    room = out.shape[-1]
    for t in range(tiles):
        piece = value[:, t * step : (t + 1) * step]
        if room > step:
            piece = jnp.concatenate([piece, jnp.zeros((n, room - step), piece.dtype)], axis=1)
        at = pl.ds(p, n, stride=count) if n > 1 else pl.ds(p, 1)
        out[(*lead, t, at, slice(None))] = piece


def mix_pair(g_high, g_low, y_re, y_im, half, sign):
    a = dot_split(g_high[...], g_low[...], y_re)
    b = dot_split(g_high[...], g_low[...], y_im)
    if sign > 0:
        return a[:half] - b[half:], b[:half] + a[half:]
    return a[:half] + b[half:], b[:half] - a[half:]


def fetch_pieces(pieces, target, sem):
    me = lax.axis_index("row")
    copies = []
    for d, piece in enumerate(pieces):
        place = target if len(pieces) == 1 else target.at[jnp.bitwise_xor(me, d)]
        copies.append(pltpu.make_async_copy(piece, place, sem.at[d]))
        copies[-1].start()
    return copies


def store_pieces(source, pieces, sem):
    me = lax.axis_index("row")
    copies = []
    for d, piece in enumerate(pieces):
        place = source if len(pieces) == 1 else source.at[jnp.bitwise_xor(me, d)]
        copies.append(pltpu.make_async_copy(place, piece, sem.at[d]))
        copies[-1].start()
    for copy in copies:
        copy.wait()


def first_kernel(count, width, kept, n, x_hbm, tw_re, tw_im, f_high, f_low, *refs):
    pieces, (x, out, y_re, y_im, x_sem, sem) = refs[:n], refs[n:]
    rows = x.shape[0]
    parts = SKY_PARTS if rows % (8 * SKY_PARTS) == 0 else 1
    copies = []
    for i in range(parts):
        at = pl.ds(i * (rows // parts), rows // parts)
        copies.append(pltpu.make_async_copy(x_hbm.at[at], x.at[at], x_sem.at[i]))
        copies[-1].start()

    def load(p, at, lanes):
        return (x[at, p * width + lanes.start : p * width + lanes.stop], None)

    def store(p, at, lanes, re, im):
        y_re[p, at, lanes] = re
        y_im[p, at, lanes] = im

    for i in range(parts):
        copies[i].wait()
        span = (i * (rows // parts), (i + 1) * (rows // parts))
        radix_stage(load, tw_re, tw_im, store, span, width, count, -1)

    def body(p, carry):
        z_re, z_im = mix_pair(f_high, f_low, y_re[p], y_im[p], count * kept, -1)
        for m in range(count):
            store_rows(out, (m, 0), p, kept, count, z_re[m * kept : (m + 1) * kept])
            store_rows(out, (m, 1), p, kept, count, z_im[m * kept : (m + 1) * kept])
        return carry

    lax.fori_loop(0, count, body, 0, unroll=UNROLL)
    store_pieces(out, pieces, sem)


def flipped(ref, at, n):
    return jnp.concatenate([ref[t, at, :].T for t in range(ref.shape[0])], axis=0)[:n]


def middle_kernel(count, width, n, *refs):
    came, refs = refs[:n], refs[n:]
    dual, vis, weights, before, tw_re, tw_im, g_high, g_low, resid, sums = refs[:10]
    pieces, refs = refs[10 : 10 + n], refs[10 + n :]
    got, out, y_re, y_im, zt_re, zt_im, s_re, s_im, sem = refs
    for copy in fetch_pieces(came, got, sem):
        copy.wait()
    batch = got.shape[3]
    length = count * width
    per = width // count

    def load(p, at, lanes):
        tile = lanes.start // got.shape[4]
        return (got[p, 0, tile, at, :], got[p, 1, tile, at, :])

    def store(p, at, lanes, re, im):
        y_re[p, at, lanes] = re
        y_im[p, at, lanes] = im

    radix_stage(load, tw_re, tw_im, store, batch, width, count, -1)

    def forward(p, carry):
        z_re, z_im = mix_pair(g_high, g_low, y_re[p], y_im[p], width, -1)
        store_rows(zt_re, (), p, width, count, z_re)
        store_rows(zt_im, (), p, width, count, z_im)
        return carry

    lax.fori_loop(0, count, forward, 0, unroll=UNROLL)

    def residual(i, carry):
        d_sum, v_sum = carry
        start = pl.multiple_of(i * 128, 128)
        at = pl.ds(start, 128)
        w = weights[0, :, at]
        v_re, v_im = vis[0, 0, :, at], vis[1, 0, :, at]
        d_re = dual[0, 0, :, at] * (1.0 / data_step) + w * flipped(zt_re, at, batch) - v_re
        d_im = dual[1, 0, :, at] * (1.0 / data_step) + w * flipped(zt_im, at, batch) - v_im
        resid[0, 0, :, at] = d_re
        resid[1, 0, :, at] = d_im
        s_re[:, at] = w * d_re
        s_im[:, at] = w * d_im
        fold = lambda t: jnp.sum(t.reshape(batch // 8, 8, 128), axis=0)
        return d_sum + fold(d_re * d_re + d_im * d_im), v_sum + fold(v_re * v_re + v_im * v_im)

    d_sum, v_sum = lax.fori_loop(0, length // 128, residual, (before[0], before[1]))
    sums[0] = d_sum
    sums[1] = v_sum

    def load_2(p, at, lanes):
        lanes = slice(p * width + lanes.start, p * width + lanes.stop)
        return (s_re[at, lanes], s_im[at, lanes])

    radix_stage(load_2, tw_re, tw_im, store, batch, width, count, 1)

    def inverse(p, carry):
        u_re, u_im = mix_pair(g_high, g_low, y_re[p], y_im[p], width, 1)
        for m in range(count):
            store_rows(out, (m, 0), p, per, count, u_re[m * per : (m + 1) * per])
            store_rows(out, (m, 1), p, per, count, u_im[m * per : (m + 1) * per])
        return carry

    lax.fori_loop(0, count, inverse, 0, unroll=UNROLL)
    store_pieces(out, pieces, sem)


def last_kernel(count, width, start, n, is_first, is_last, *refs):
    came, refs = refs[:n], list(refs[n:])
    take = lambda k: [refs.pop(0) for _ in range(k)]
    base_hbm = take(3 if is_first else 1)
    tw_re, tw_im, g_high, g_low, shrink, out_hbm, got, base, y_re, y_im, gt, sem, came_sem = take(13)
    adjoint = refs.pop(0) if is_first else None
    rows, batch = got.shape[3], got.shape[2] * got.shape[4]
    length = count * width
    me = lax.axis_index("chan")
    fetch_got = fetch_pieces(came, got, came_sem)
    half = rows // 2
    fetch_base = [pltpu.make_async_copy(base_hbm[0], base, sem.at[0])]
    if is_first:
        for i, side in enumerate((me, 1 - me)):
            place = adjoint.at[pl.ds(pl.multiple_of(half * side, 8), half)]
            fetch_base.append(pltpu.make_async_copy(base_hbm[1 + i], place, sem.at[1 + i]))
    for copy in fetch_base:
        copy.start()
    for copy in fetch_got:
        copy.wait()

    def load(p, at, lanes):
        tile = lanes.start // got.shape[4]
        return (got[p, 0, tile, at, :], got[p, 1, tile, at, :])

    def store(p, at, lanes, re, im):
        y_re[p, at, lanes] = re
        y_im[p, at, lanes] = im

    radix_stage(load, tw_re, tw_im, store, rows, batch, count, 1, start)
    cols = slice(start, start + batch)
    e_high = jnp.concatenate([g_high[:width, cols], -g_high[width:, cols]], axis=1)
    e_low = jnp.concatenate([g_low[:width, cols], -g_low[width:, cols]], axis=1)

    def inverse(p, carry):
        u = dot_split(e_high, e_low, jnp.concatenate([y_re[p], y_im[p]], axis=1))
        store_rows(gt, (), p, width, count, u)
        return carry

    lax.fori_loop(0, count, inverse, 0, unroll=UNROLL)
    for copy in fetch_base:
        copy.wait()
    scale = primal_step * shrink[0]
    groups = 4
    stores = []
    for g in range(groups):
        tiles = length // 128 // groups

        def finish(i, carry):
            at = pl.ds(pl.multiple_of(i * 128, 128), 128)
            value = base[:, at] - scale * flipped(gt, at, rows)
            if is_first:
                value = value - primal_step * adjoint[:, at]
            base[:, at] = jnp.maximum(value, 0.0) if is_last else value
            return carry

        lax.fori_loop(g * tiles, (g + 1) * tiles, finish, 0, unroll=UNROLL)
        at = pl.ds(g * tiles * 128, tiles * 128)
        stores.append(pltpu.make_async_copy(base.at[:, at], out_hbm.at[:, at], sem.at[3 + g]))
        stores[-1].start()
    for copy in stores:
        copy.wait()


def vmem(shape, dtype=jnp.float32):
    return pltpu.VMEM(shape, dtype)


def whole(shape):
    return pl.BlockSpec(shape, lambda *_: (0,) * len(shape), pipeline_mode=pl.Buffered(1))


def call(kernel, args, specs, out_shape, out_specs, scratch, flops, moved):
    return pl.pallas_call(
        kernel,
        grid=(1,),
        in_specs=specs,
        out_specs=out_specs,
        out_shape=out_shape,
        scratch_shapes=scratch,
        cost_estimate=pl.CostEstimate(flops=flops, bytes_accessed=moved, transcendentals=0),
        compiler_params=pltpu.CompilerParams(vmem_limit_bytes=VMEM_LIMIT),
    )(*args)


def analysis(source, start, n, low, high):
    if isinstance(start, int):
        taps = [source[start + p : start + p + n, :] for p in range(5)]
    else:
        window = source[pl.ds(pl.multiple_of(start - 6, 8), n + 16), :]
        taps = [window[6 + p : 6 + p + n] for p in range(5)]
    width = taps[0].shape[1]

    def along(coefs):
        if coefs[0] == coefs[4]:
            total = coefs[2] * taps[2] + coefs[0] * (taps[0] + taps[4])
        else:
            total = coefs[2] * taps[2] + (coefs[0] * taps[0] + coefs[4] * taps[4])
        if coefs[1] == coefs[3]:
            return total + coefs[1] * (taps[1] + taps[3])
        return total + (coefs[1] * taps[1] + coefs[3] * taps[3])

    a, b = along(high), along(low)
    total = low[2] * a + high[2] * b
    pad = jnp.zeros((n, 128), jnp.float32)
    mixed = {}
    for p in (0, 1, 3, 4):
        pair = (low[p], high[p])
        if pair not in mixed:
            mixed[pair] = jnp.concatenate([low[p] * a + high[p] * b, pad], axis=1)
        total = total + pltpu.roll(mixed[pair], (2 - p) % (width + 128), 1)[:, :width]
    return total


def wave_kernel(
    count, sky, other, edge_own, edge_other, dual, above, below, limit, wave, outside, x, sem
):
    me = lax.axis_index("chan")
    row = lax.axis_index("row")
    half = limit.shape[0]
    base = pl.multiple_of(8 * (1 - me), 8)
    edge = pl.ds(pl.multiple_of((half + 8) * me, 8), 8)
    own_rows = pl.ds(pl.multiple_of((half - 8) * me, 8), half + 8)
    copies = [
        pltpu.make_async_copy(sky.at[own_rows], x.at[0, pl.ds(base, half + 8)], sem.at[0]),
        pltpu.make_async_copy(other, x.at[1, pl.ds(base, half + 8)], sem.at[1]),
        pltpu.make_async_copy(edge_own, x.at[0, edge], sem.at[2]),
        pltpu.make_async_copy(edge_other, x.at[1, edge], sem.at[3]),
    ]
    for copy in copies:
        copy.start()
    for copy in copies:
        copy.wait()

    def shrunk(start, n, dual_own, dual_other, bound):
        s_own = dual_own + analysis(x.at[0], start - 2, n, low_taps, high_taps)
        s_other = dual_other + analysis(x.at[1], start - 2, n, low_taps, high_taps)
        factor = bound / jnp.maximum(jnp.sqrt(s_own * s_own + s_other * s_other), bound)
        return s_own * factor, s_other * factor

    first = jnp.logical_and(row == 0, me == 0)
    last = jnp.logical_and(row == count - 1, me == 1)
    outside[...] = jnp.zeros_like(outside)
    for side, (ref, start, beyond) in enumerate(((above, 6, first), (below, half + 8, last))):
        a, b = shrunk(start, 2, ref[me], ref[1 - me], ref[2])
        at = slice(6, 8) if side == 0 else slice(0, 2)
        outside[0, side, at, :] = jnp.where(beyond, 0.0, a)
        outside[1, side, at, :] = jnp.where(beyond, 0.0, b)

    def body(i, carry):
        at = pl.ds(pl.multiple_of(i * 8, 8), 8)
        a, b = shrunk(i * 8 + 8, 8, dual[me, at, :], dual[1 - me, at, :], limit[at, :])
        wave[me, at, :] = a
        wave[1 - me, at, :] = b
        return carry

    lax.fori_loop(0, half // 8, body, 0)


def adjoint_kernel(wave, outside, own_out, other_out, w, sem):
    me = lax.axis_index("chan")
    half = own_out.shape[0]
    copies = []
    for i, plane in enumerate((me, 1 - me)):
        copies.append(pltpu.make_async_copy(wave.at[plane], w.at[i, pl.ds(8, half)], sem.at[i, 0]))
        copies.append(pltpu.make_async_copy(outside.at[i, 0], w.at[i, pl.ds(0, 8)], sem.at[i, 1]))
        copies.append(pltpu.make_async_copy(outside.at[i, 1], w.at[i, pl.ds(half + 8, 8)], sem.at[i, 2]))
    for copy in copies:
        copy.start()
    for copy in copies:
        copy.wait()

    def back(i, carry):
        at = pl.ds(pl.multiple_of(i * 8, 8), 8)
        own_out[at, :] = analysis(w.at[0], i * 8 + 6, 8, low_reverse, high_reverse)
        other_out[at, :] = analysis(w.at[1], i * 8 + 6, 8, low_reverse, high_reverse)
        return carry

    lax.fori_loop(0, half // 8, back, 0)


def chan_swap(value):
    size = lax.axis_size("chan")
    return lax.ppermute(value, "chan", [(i, (i + 1) % size) for i in range(size)])


UNROLL = 4
SKY_PARTS = 4


def partners(size):
    quarter = size // 4
    far = [d for i in range(quarter) for d in (2 * quarter + i, 3 * quarter + i)]
    return far[:2] + [*range(quarter, 2 * quarter), *range(1, quarter)] + far[2:]


def row_exchange(pieces):
    if len(pieces) == 1:
        return [lax.all_to_all(pieces[0], "row", split_axis=0, concat_axis=0, tiled=True)]
    size = len(pieces)
    got = list(pieces)
    for d in reversed(partners(size)):
        got[d] = lax.ppermute(pieces[d], "row", [(i, i ^ d) for i in range(size)])
    return got


def row_total(value):
    size = lax.axis_size("row")
    away = lambda v, d: lax.ppermute(v, "row", [(i, i ^ d) for i in range(size)])
    step = 1
    while step < size // 4:
        value = value + away(value, step)
        step *= 2
    return value + (away(value, step) + away(value, 2 * step)) + away(value, 3 * step)


def edges_of(sky):
    count, size = lax.axis_size("row"), lax.axis_size("chan")
    top, bottom = sky[:8], sky[-8:]
    me = lax.axis_index("chan")
    at = lambda r, c: r * size + c
    own = [(at(r, 0), at(r + 1, 0)) for r in range(count - 1)] + [(at(r + 1, 1), at(r, 1)) for r in range(count - 1)]
    cross = [(at(r, 1), at(r + 1, 0)) for r in range(count - 1)] + [(at(r + 1, 0), at(r, 1)) for r in range(count - 1)]
    sent_own = jnp.where(me == 0, bottom, top)
    sent_cross = jnp.where(me == 0, top, bottom)
    axes = ("row", "chan")
    return lax.ppermute(sent_own, axes, own), lax.ppermute(sent_cross, axes, cross)


def facet_neighbours(wavelet_dual, reweight):
    axes = ("row", "chan")
    count = lax.axis_size(axes)
    up = [(i, i + 1) for i in range(count - 1)]
    down = [(j, i) for i, j in up]
    last = jnp.concatenate([wavelet_dual[:, -2:], reweight[None, -2:]])
    first = jnp.concatenate([wavelet_dual[:, :2], reweight[None, :2]])
    return lax.ppermute(last, axes, up), lax.ppermute(first, axes, down)


def per_device(sky_image, fourier_dual, visibilities, weights, radius, wavelet_dual, reweight):
    f32 = jnp.float32
    sky = sky_image[0]
    rows, length = sky.shape
    count = lax.axis_size("row")
    width = length // count
    per = width // count
    chunks = 2 if per % 2 == 0 else 1
    batch = width // chunks
    kept = per // chunks
    scale = 1.0 / math.sqrt(length)
    shape = jax.ShapeDtypeStruct

    any_space = pl.BlockSpec(memory_space=pl.ANY)
    dma = lambda n: pltpu.SemaphoreType.DMA((n,))
    n = count if count & (count - 1) == 0 and count <= 16 else 1
    pieces_of = lambda packed: [shape(packed[1:], f32)] * n if n > 1 else [shape(packed, f32)]

    def tile(high, wide):
        tiles, step = lane_tiles(wide)
        return tiles, high, step

    lanes = np.arange(width)
    tw = phase_rows(count, lanes, length)
    g_table = split_constant(scale * np.concatenate(dft_matrix(lanes, lanes, width, 1)))

    sent = []
    for c in range(chunks):
        picked = (np.arange(count)[:, None] * per + c * kept + np.arange(kept)[None, :]).reshape(-1)
        table = split_constant(scale * np.concatenate(dft_matrix(picked, lanes, width, 1)))
        args = (sky, *tw, *table)
        packed = (count, 2, *tile(batch, rows))
        piece = call(
            partial(first_kernel, count, width, kept, n), args,
            [any_space] + [whole(a.shape) for a in args[1:]], pieces_of(packed), [any_space] * n,
            [vmem(sky.shape), vmem(packed)] + [vmem((count, rows, width))] * 2 + [dma(SKY_PARTS), dma(n)],
            10**10, 10**7,
        )
        sent.append(row_exchange(piece))

    half = rows // 2
    me = lax.axis_index("chan")
    theirs = lax.dynamic_slice_in_dim(sky, (1 - me) * (half - 8), half + 8, 0)
    other = chan_swap(theirs)
    edge_own, edge_other = edges_of(sky)
    above, below = facet_neighbours(wavelet_dual, reweight)
    args = (sky, other, edge_own, edge_other, wavelet_dual, above, below, reweight)
    outs = (shape((2, half, length), f32), shape((2, 2, 8, length), f32))
    wavelet_new, outside = call(
        partial(wave_kernel, count), args, [any_space] * 4 + [whole(a.shape) for a in args[4:]],
        outs, tuple(whole(o.shape) for o in outs),
        [vmem((2, half + 16, length)), dma(4)], 10**10, 3 * 10**7,
    )
    outs = (shape((half, length), f32), shape((half, length), f32))
    adjoint_own, adjoint_other = call(
        adjoint_kernel, (wavelet_new, outside), [any_space] * 2, outs, tuple(whole(o.shape) for o in outs),
        [vmem((2, half + 16, length)), pltpu.SemaphoreType.DMA((2, 3))], 10**10, 3 * 10**7,
    )
    adjoint_got = chan_swap(adjoint_other)

    resid, returned, sums = [], [], np.zeros((2, 8, 128), np.float32)
    for c in range(chunks):
        block = lambda lead, c=c: pl.BlockSpec(
            (*lead, batch, length), lambda i: (0,) * len(lead) + (c, 0), pipeline_mode=pl.Buffered(1)
        )
        tables = (*tw, *g_table)
        coming = (count, 2, *tile(batch, rows))
        packed = (count, 2, *tile(rows, batch))
        outs = (shape((2, 1, batch, length), f32), shape((2, 8, 128), f32))
        d, part, *piece = call(
            partial(middle_kernel, count, width, n),
            (*sent[c], fourier_dual, visibilities, weights, sums, *tables),
            [any_space] * n + [block((2, 1)), block((2, 1)), block((1,)), *(whole(t.shape) for t in (sums, *tables))],
            [*outs, *pieces_of(packed)], [whole(o.shape) for o in outs] + [any_space] * n,
            [vmem(coming), vmem(packed)] + [vmem((count, batch, width))] * 2 + [vmem((-(-batch // 128), length, 128))] * 2 + [vmem((batch, length))] * 2 + [dma(n)],
            2 * 10**10, 3 * 10**7,
        )
        resid.append(d)
        sums = part
        returned.append(row_exchange(piece))

    total = row_total(sums) if n > 1 else lax.psum(sums, "row")
    data_norm = jnp.sum(total[1])
    resid_norm = jnp.sum(total[0])
    shrink = data_step * (1.0 - radius * jnp.sqrt(data_norm) / jnp.sqrt(resid_norm))
    fourier_new = jnp.concatenate([d * shrink for d in resid], axis=2)

    base = (sky, adjoint_own, adjoint_got)
    for c in range(chunks):
        packed = (count, 2, *tile(rows, batch))
        args = (*returned[c], *base, *tw, *g_table, shrink)
        specs = [any_space] * (n + len(base)) + [whole(a.shape) for a in (*tw, *g_table)]
        specs.append(pl.BlockSpec(memory_space=pltpu.SMEM))
        scratch = [
            vmem(packed), vmem((rows, length)), *[vmem((count, rows, batch))] * 2,
            vmem((-(-rows // 128), length, 128)), dma(7), dma(n), *[vmem((rows, length))] * (c == 0),
        ]
        image_new = call(
            partial(last_kernel, count, width, c * batch, n, c == 0, c == chunks - 1), args, specs,
            shape((rows, length), f32), any_space, scratch, 10**10, 3 * 10**7,
        )
        base = (image_new,)
    return (image_new[None], fourier_new, wavelet_new)


def solution(mesh):
    in_specs = (
        P("chan", "row", None),
        P(None, "chan", "row", None),
        P(None, "chan", "row", None),
        P("chan", "row", None),
        P("chan"),
        P(None, ("row", "chan"), None),
        P(("row", "chan"), None),
    )
    out_specs = (
        P("chan", "row", None),
        P(None, "chan", "row", None),
        P(None, ("row", "chan"), None),
    )

    return jax.shard_map(per_device, mesh=mesh, in_specs=in_specs, out_specs=out_specs, check_vma=False)
```

```python
import math
from functools import partial

import jax
import jax.numpy as jnp
import ml_dtypes
import numpy as np
from jax import lax
from jax.experimental import pallas as pl
from jax.experimental.pallas import tpu as pltpu
from jax.sharding import PartitionSpec as P


data_step = 0.8
primal_step = 0.5
low_taps = (0.0625, 0.25, 0.375, 0.25, 0.0625)
high_taps = (-0.1, -0.3, 0.7, -0.2, -0.1)
low_reverse = (0.0625, 0.25, 0.375, 0.25, 0.0625)
high_reverse = (-0.1, -0.2, 0.7, -0.3, -0.1)

VMEM_LIMIT = 60 * 1024 * 1024


def c_add(x, y):
    if x[1] is None and y[1] is None:
        return (x[0] + y[0], None)
    if x[1] is None:
        return (x[0] + y[0], y[1])
    if y[1] is None:
        return (x[0] + y[0], x[1])
    return (x[0] + y[0], x[1] + y[1])


def c_sub(x, y):
    if x[1] is None and y[1] is None:
        return (x[0] - y[0], None)
    if x[1] is None:
        return (x[0] - y[0], -y[1])
    if y[1] is None:
        return (x[0] - y[0], x[1])
    return (x[0] - y[0], x[1] - y[1])


def c_rot(x, turn):
    turn = turn % 1.0
    wr, wi = math.cos(2 * math.pi * turn), math.sin(2 * math.pi * turn)
    re, im = x
    if turn == 0.0:
        return x
    if turn == 0.5:
        return (-re, None if im is None else -im)
    if turn == 0.25:
        return (jnp.zeros_like(re) if im is None else -im, re)
    if turn == 0.75:
        return (jnp.zeros_like(re) if im is None else im, -re)
    if im is None:
        return (re * wr, re * wi)
    if abs(abs(wr) - abs(wi)) < 1e-12:
        h = abs(wr)
        p, m = (re + im) * h, (re - im) * h
        if wr > 0:
            return (m, p) if wi > 0 else (p, -m)
        return (-p, m) if wi > 0 else (-m, -p)
    return (re * wr - im * wi, re * wi + im * wr)


def c_rot90_add(x, y, sign):
    re, im = x
    yr, yi = y
    if yi is not None:
        re = re - yi if sign > 0 else re + yi
    if im is None:
        im = yr if sign > 0 else -yr
    else:
        im = im + yr if sign > 0 else im - yr
    return (re, im)


def small_dft(xs, sign):
    n = len(xs)
    if n == 1:
        return list(xs)
    if n == 2:
        return [c_add(xs[0], xs[1]), c_sub(xs[0], xs[1])]
    if n % 4 == 0:
        parts = [small_dft(xs[r::4], sign) for r in range(4)]
        out = [None] * n
        for k in range(n // 4):
            t = [c_rot(parts[r][k], sign * r * k / n) for r in range(4)]
            s0, s1 = c_add(t[0], t[2]), c_sub(t[0], t[2])
            s2, s3 = c_add(t[1], t[3]), c_sub(t[1], t[3])
            out[k] = c_add(s0, s2)
            out[k + n // 2] = c_sub(s0, s2)
            out[k + n // 4] = c_rot90_add(s1, s3, sign)
            out[k + 3 * n // 4] = c_rot90_add(s1, s3, -sign)
        return out
    even, odd = small_dft(xs[0::2], sign), small_dft(xs[1::2], sign)
    out = [None] * n
    for k in range(n // 2):
        t = c_rot(odd[k], sign * k / n)
        out[k], out[k + n // 2] = c_add(even[k], t), c_sub(even[k], t)
    return out


def split_constant(table):
    high = table.astype(ml_dtypes.bfloat16)
    low = (table - high.astype(np.float64)).astype(ml_dtypes.bfloat16)
    return high, low


def dft_matrix(rows, cols, length, sign):
    angle = 2.0 * np.pi * ((np.asarray(rows)[:, None] * np.asarray(cols)[None, :]) % length) / length
    return np.cos(angle), sign * np.sin(angle)


def phase_rows(count, positions, length):
    wide = lambda t: np.ascontiguousarray(np.broadcast_to(t[:, None, :], (count, 8, t.shape[1]))).astype(np.float32)
    re, im = dft_matrix(np.arange(count), positions, length, 1)
    return wide(re), wide(im)


def split_value(value):
    high = value.astype(jnp.bfloat16)
    low = (value - high.astype(jnp.float32)).astype(jnp.bfloat16)
    return high, low


def dot_nt(a, b):
    return lax.dot_general(a, b, (((1,), (1,)), ((), ())), preferred_element_type=jnp.float32)


def dot_split(high, low, value):
    v_high, v_low = split_value(value)
    return dot_nt(high, v_high) + (dot_nt(low, v_high) + dot_nt(high, v_low))


def lane_step(width):
    return 128 if width % 128 == 0 else width


def radix_stage(load, tw_re, tw_im, store, rows, width, count, sign, shift=0):
    step = lane_step(width)
    low, high = rows if isinstance(rows, tuple) else (0, rows)

    def body(i, carry):
        at = pl.ds(pl.multiple_of(i * 8, 8), 8)
        for lane in range(0, width, step):
            lanes = slice(lane, lane + step)
            ys = small_dft([load(p, at, lanes) for p in range(count)], sign)
            for p in range(count):
                re, im = ys[p]
                if p == 0:
                    store(p, at, lanes, re, jnp.zeros_like(re) if im is None else im)
                    continue
                from_table = slice(shift + lane, shift + lane + step)
                wr, wi = tw_re[p, :, from_table], tw_im[p, :, from_table]
                if im is None:
                    store(p, at, lanes, re * wr, re * wi if sign > 0 else -(re * wi))
                elif sign > 0:
                    store(p, at, lanes, re * wr - im * wi, re * wi + im * wr)
                else:
                    store(p, at, lanes, re * wr + im * wi, im * wr - re * wi)
        return carry

    lax.fori_loop(low // 8, high // 8, body, 0, unroll=2)


def lane_tiles(width):
    step = lane_step(width)
    return width // step, step


def store_rows(out, lead, p, n, count, value):
    tiles, step = lane_tiles(value.shape[1])
    room = out.shape[-1]
    for t in range(tiles):
        piece = value[:, t * step : (t + 1) * step]
        if room > step:
            piece = jnp.concatenate([piece, jnp.zeros((n, room - step), piece.dtype)], axis=1)
        at = pl.ds(p, n, stride=count) if n > 1 else pl.ds(p, 1)
        out[(*lead, t, at, slice(None))] = piece


def mix_pair(g_high, g_low, y_re, y_im, half, sign):
    a = dot_split(g_high[...], g_low[...], y_re)
    b = dot_split(g_high[...], g_low[...], y_im)
    if sign > 0:
        return a[:half] - b[half:], b[:half] + a[half:]
    return a[:half] + b[half:], b[:half] - a[half:]


def fetch_spans(pieces, target, sem, spans):
    me = lax.axis_index("row")
    rows = target.shape[3] // spans
    starts = []
    for i in range(spans):
        at = pl.ds(i * rows, rows)
        copies = []
        for d, piece in enumerate(pieces):
            if len(pieces) == 1:
                source, place = piece.at[:, :, :, at], target.at[:, :, :, at]
            else:
                source, place = piece.at[:, :, at], target.at[jnp.bitwise_xor(me, d), :, :, at]
            copies.append(pltpu.make_async_copy(source, place, sem.at[i * len(pieces) + d]))
            copies[-1].start()
        starts.append(copies)
    return starts


def fetch_pieces(pieces, target, sem):
    me = lax.axis_index("row")
    copies = []
    for d, piece in enumerate(pieces):
        place = target if len(pieces) == 1 else target.at[jnp.bitwise_xor(me, d)]
        copies.append(pltpu.make_async_copy(piece, place, sem.at[d]))
        copies[-1].start()
    return copies


def store_pieces(source, pieces, sem):
    me = lax.axis_index("row")
    copies = []
    for d, piece in enumerate(pieces):
        place = source if len(pieces) == 1 else source.at[jnp.bitwise_xor(me, d)]
        copies.append(pltpu.make_async_copy(place, piece, sem.at[d]))
        copies[-1].start()
    for copy in copies:
        copy.wait()


def first_kernel(count, width, kept, n, x_hbm, tw_re, tw_im, f_high, f_low, *refs):
    pieces, (x, out, y_re, y_im, x_sem, sem) = refs[:n], refs[n:]
    rows = x.shape[0]
    parts = SKY_PARTS if rows % (8 * SKY_PARTS) == 0 else 1
    copies = []
    for i in range(parts):
        at = pl.ds(i * (rows // parts), rows // parts)
        copies.append(pltpu.make_async_copy(x_hbm.at[at], x.at[at], x_sem.at[i]))
        copies[-1].start()

    def load(p, at, lanes):
        return (x[at, p * width + lanes.start : p * width + lanes.stop], None)

    def store(p, at, lanes, re, im):
        y_re[p, at, lanes] = re
        y_im[p, at, lanes] = im

    for i in range(parts):
        copies[i].wait()
        span = (i * (rows // parts), (i + 1) * (rows // parts))
        radix_stage(load, tw_re, tw_im, store, span, width, count, -1)

    def body(p, carry):
        z_re, z_im = mix_pair(f_high, f_low, y_re[p], y_im[p], count * kept, -1)
        for m in range(count):
            store_rows(out, (m, 0), p, kept, count, z_re[m * kept : (m + 1) * kept])
            store_rows(out, (m, 1), p, kept, count, z_im[m * kept : (m + 1) * kept])
        return carry

    lax.fori_loop(0, count, body, 0, unroll=UNROLL)
    store_pieces(out, pieces, sem)


def flipped(ref, at, n):
    return jnp.concatenate([ref[t, at, :].T for t in range(ref.shape[0])], axis=0)[:n]


def middle_kernel(count, width, n, *refs):
    came, refs = refs[:n], refs[n:]
    dual, vis, weights, before, tw_re, tw_im, g_high, g_low, resid, sums = refs[:10]
    pieces, refs = refs[10 : 10 + n], refs[10 + n :]
    got, out, y_re, y_im, zt_re, zt_im, s_re, s_im, sem = refs
    for copy in fetch_pieces(came, got, sem):
        copy.wait()
    batch = got.shape[3]
    length = count * width
    per = width // count

    def load(p, at, lanes):
        tile = lanes.start // got.shape[4]
        return (got[p, 0, tile, at, :], got[p, 1, tile, at, :])

    def store(p, at, lanes, re, im):
        y_re[p, at, lanes] = re
        y_im[p, at, lanes] = im

    radix_stage(load, tw_re, tw_im, store, batch, width, count, -1)

    def forward(p, carry):
        z_re, z_im = mix_pair(g_high, g_low, y_re[p], y_im[p], width, -1)
        store_rows(zt_re, (), p, width, count, z_re)
        store_rows(zt_im, (), p, width, count, z_im)
        return carry

    lax.fori_loop(0, count, forward, 0, unroll=UNROLL)

    def residual(i, carry):
        d_sum, v_sum = carry
        start = pl.multiple_of(i * 128, 128)
        at = pl.ds(start, 128)
        w = weights[0, :, at]
        v_re, v_im = vis[0, 0, :, at], vis[1, 0, :, at]
        d_re = dual[0, 0, :, at] * (1.0 / data_step) + w * flipped(zt_re, at, batch) - v_re
        d_im = dual[1, 0, :, at] * (1.0 / data_step) + w * flipped(zt_im, at, batch) - v_im
        resid[0, 0, :, at] = d_re
        resid[1, 0, :, at] = d_im
        s_re[:, at] = w * d_re
        s_im[:, at] = w * d_im
        fold = lambda t: jnp.sum(t.reshape(batch // 8, 8, 128), axis=0)
        return d_sum + fold(d_re * d_re + d_im * d_im), v_sum + fold(v_re * v_re + v_im * v_im)

    d_sum, v_sum = lax.fori_loop(0, length // 128, residual, (before[0], before[1]))
    sums[0] = d_sum
    sums[1] = v_sum

    def load_2(p, at, lanes):
        lanes = slice(p * width + lanes.start, p * width + lanes.stop)
        return (s_re[at, lanes], s_im[at, lanes])

    radix_stage(load_2, tw_re, tw_im, store, batch, width, count, 1)

    def inverse(p, carry):
        u_re, u_im = mix_pair(g_high, g_low, y_re[p], y_im[p], width, 1)
        for m in range(count):
            store_rows(out, (m, 0), p, per, count, u_re[m * per : (m + 1) * per])
            store_rows(out, (m, 1), p, per, count, u_im[m * per : (m + 1) * per])
        return carry

    lax.fori_loop(0, count, inverse, 0, unroll=UNROLL)
    store_pieces(out, pieces, sem)


def last_kernel(count, width, start, n, is_first, is_last, *refs):
    came, refs = refs[:n], list(refs[n:])
    take = lambda k: [refs.pop(0) for _ in range(k)]
    base_hbm = take(3 if is_first else 1)
    tw_re, tw_im, g_high, g_low, shrink, out_hbm, got, base, y_re, y_im, gt, sem, came_sem = take(13)
    adjoint = refs.pop(0) if is_first else None
    rows, batch = got.shape[3], got.shape[2] * got.shape[4]
    length = count * width
    me = lax.axis_index("chan")
    spans = GOT_PARTS if rows % (8 * GOT_PARTS) == 0 else 1
    fetch_got = fetch_spans(came, got, came_sem, spans)
    half = rows // 2
    fetch_base = [pltpu.make_async_copy(base_hbm[0], base, sem.at[0])]
    if is_first:
        for i, side in enumerate((me, 1 - me)):
            place = adjoint.at[pl.ds(pl.multiple_of(half * side, 8), half)]
            fetch_base.append(pltpu.make_async_copy(base_hbm[1 + i], place, sem.at[1 + i]))
    for copy in fetch_base:
        copy.start()

    def load(p, at, lanes):
        tile = lanes.start // got.shape[4]
        return (got[p, 0, tile, at, :], got[p, 1, tile, at, :])

    def store(p, at, lanes, re, im):
        y_re[p, at, lanes] = re
        y_im[p, at, lanes] = im

    for i in range(spans):
        for copy in fetch_got[i]:
            copy.wait()
        span = (i * (rows // spans), (i + 1) * (rows // spans))
        radix_stage(load, tw_re, tw_im, store, span, batch, count, 1, start)
    cols = slice(start, start + batch)
    e_high = jnp.concatenate([g_high[:width, cols], -g_high[width:, cols]], axis=1)
    e_low = jnp.concatenate([g_low[:width, cols], -g_low[width:, cols]], axis=1)

    def inverse(p, carry):
        u = dot_split(e_high, e_low, jnp.concatenate([y_re[p], y_im[p]], axis=1))
        store_rows(gt, (), p, width, count, u)
        return carry

    lax.fori_loop(0, count, inverse, 0, unroll=UNROLL)
    for copy in fetch_base:
        copy.wait()
    scale = primal_step * shrink[0]
    groups = 4
    stores = []
    for g in range(groups):
        tiles = length // 128 // groups

        def finish(i, carry):
            at = pl.ds(pl.multiple_of(i * 128, 128), 128)
            value = base[:, at] - scale * flipped(gt, at, rows)
            if is_first:
                value = value - primal_step * adjoint[:, at]
            base[:, at] = jnp.maximum(value, 0.0) if is_last else value
            return carry

        lax.fori_loop(g * tiles, (g + 1) * tiles, finish, 0, unroll=UNROLL)
        at = pl.ds(g * tiles * 128, tiles * 128)
        stores.append(pltpu.make_async_copy(base.at[:, at], out_hbm.at[:, at], sem.at[3 + g]))
        stores[-1].start()
    for copy in stores:
        copy.wait()


def vmem(shape, dtype=jnp.float32):
    return pltpu.VMEM(shape, dtype)


def whole(shape):
    return pl.BlockSpec(shape, lambda *_: (0,) * len(shape), pipeline_mode=pl.Buffered(1))


def call(kernel, args, specs, out_shape, out_specs, scratch, flops, moved):
    return pl.pallas_call(
        kernel,
        grid=(1,),
        in_specs=specs,
        out_specs=out_specs,
        out_shape=out_shape,
        scratch_shapes=scratch,
        cost_estimate=pl.CostEstimate(flops=flops, bytes_accessed=moved, transcendentals=0),
        compiler_params=pltpu.CompilerParams(vmem_limit_bytes=VMEM_LIMIT),
    )(*args)


def analysis(source, start, n, low, high):
    if isinstance(start, int):
        taps = [source[start + p : start + p + n, :] for p in range(5)]
    else:
        window = source[pl.ds(pl.multiple_of(start - 6, 8), n + 16), :]
        taps = [window[6 + p : 6 + p + n] for p in range(5)]
    width = taps[0].shape[1]

    def along(coefs):
        if coefs[0] == coefs[4]:
            total = coefs[2] * taps[2] + coefs[0] * (taps[0] + taps[4])
        else:
            total = coefs[2] * taps[2] + (coefs[0] * taps[0] + coefs[4] * taps[4])
        if coefs[1] == coefs[3]:
            return total + coefs[1] * (taps[1] + taps[3])
        return total + (coefs[1] * taps[1] + coefs[3] * taps[3])

    a, b = along(high), along(low)
    total = low[2] * a + high[2] * b
    pad = jnp.zeros((n, 128), jnp.float32)
    mixed = {}
    for p in (0, 1, 3, 4):
        pair = (low[p], high[p])
        if pair not in mixed:
            mixed[pair] = jnp.concatenate([low[p] * a + high[p] * b, pad], axis=1)
        total = total + pltpu.roll(mixed[pair], (2 - p) % (width + 128), 1)[:, :width]
    return total


def wave_kernel(
    count, sky, other, edge_own, edge_other, dual, above, below, limit, wave, outside, x, sem
):
    me = lax.axis_index("chan")
    row = lax.axis_index("row")
    half = limit.shape[0]
    base = pl.multiple_of(8 * (1 - me), 8)
    edge = pl.ds(pl.multiple_of((half + 8) * me, 8), 8)
    own_rows = pl.ds(pl.multiple_of((half - 8) * me, 8), half + 8)
    copies = [
        pltpu.make_async_copy(sky.at[own_rows], x.at[0, pl.ds(base, half + 8)], sem.at[0]),
        pltpu.make_async_copy(other, x.at[1, pl.ds(base, half + 8)], sem.at[1]),
        pltpu.make_async_copy(edge_own, x.at[0, edge], sem.at[2]),
        pltpu.make_async_copy(edge_other, x.at[1, edge], sem.at[3]),
    ]
    for copy in copies:
        copy.start()
    for copy in copies:
        copy.wait()

    def shrunk(start, n, dual_own, dual_other, bound):
        s_own = dual_own + analysis(x.at[0], start - 2, n, low_taps, high_taps)
        s_other = dual_other + analysis(x.at[1], start - 2, n, low_taps, high_taps)
        factor = bound / jnp.maximum(jnp.sqrt(s_own * s_own + s_other * s_other), bound)
        return s_own * factor, s_other * factor

    first = jnp.logical_and(row == 0, me == 0)
    last = jnp.logical_and(row == count - 1, me == 1)
    outside[...] = jnp.zeros_like(outside)
    for side, (ref, start, beyond) in enumerate(((above, 6, first), (below, half + 8, last))):
        a, b = shrunk(start, 2, ref[me], ref[1 - me], ref[2])
        at = slice(6, 8) if side == 0 else slice(0, 2)
        outside[0, side, at, :] = jnp.where(beyond, 0.0, a)
        outside[1, side, at, :] = jnp.where(beyond, 0.0, b)

    def body(i, carry):
        at = pl.ds(pl.multiple_of(i * 8, 8), 8)
        a, b = shrunk(i * 8 + 8, 8, dual[me, at, :], dual[1 - me, at, :], limit[at, :])
        wave[me, at, :] = a
        wave[1 - me, at, :] = b
        return carry

    lax.fori_loop(0, half // 8, body, 0)


def adjoint_kernel(wave, outside, own_out, other_out, w, sem):
    me = lax.axis_index("chan")
    half = own_out.shape[0]
    copies = []
    for i, plane in enumerate((me, 1 - me)):
        copies.append(pltpu.make_async_copy(wave.at[plane], w.at[i, pl.ds(8, half)], sem.at[i, 0]))
        copies.append(pltpu.make_async_copy(outside.at[i, 0], w.at[i, pl.ds(0, 8)], sem.at[i, 1]))
        copies.append(pltpu.make_async_copy(outside.at[i, 1], w.at[i, pl.ds(half + 8, 8)], sem.at[i, 2]))
    for copy in copies:
        copy.start()
    for copy in copies:
        copy.wait()

    def back(i, carry):
        at = pl.ds(pl.multiple_of(i * 8, 8), 8)
        own_out[at, :] = analysis(w.at[0], i * 8 + 6, 8, low_reverse, high_reverse)
        other_out[at, :] = analysis(w.at[1], i * 8 + 6, 8, low_reverse, high_reverse)
        return carry

    lax.fori_loop(0, half // 8, back, 0)


def chan_swap(value):
    size = lax.axis_size("chan")
    return lax.ppermute(value, "chan", [(i, (i + 1) % size) for i in range(size)])


UNROLL = 4
SKY_PARTS = 4
GOT_PARTS = 2


def partners(size):
    quarter = size // 4
    far = [d for i in range(quarter) for d in (2 * quarter + i, 3 * quarter + i)]
    near, half = list(range(quarter, 2 * quarter)), quarter // 2
    return far[:2] + near[:half] + far[2:4] + near[half:] + far[4:6] + [*range(1, quarter)] + far[6:]


def row_exchange(pieces):
    if len(pieces) == 1:
        return [lax.all_to_all(pieces[0], "row", split_axis=0, concat_axis=0, tiled=True)]
    size = len(pieces)
    got = list(pieces)
    for d in reversed(partners(size)):
        got[d] = lax.ppermute(pieces[d], "row", [(i, i ^ d) for i in range(size)])
    return got


def row_total(value):
    size = lax.axis_size("row")
    away = lambda v, d: lax.ppermute(v, "row", [(i, i ^ d) for i in range(size)])
    step = 1
    while step < size // 4:
        value = value + away(value, step)
        step *= 2
    return value + (away(value, step) + away(value, 2 * step)) + away(value, 3 * step)


def edges_of(sky):
    count, size = lax.axis_size("row"), lax.axis_size("chan")
    top, bottom = sky[:8], sky[-8:]
    me = lax.axis_index("chan")
    at = lambda r, c: r * size + c
    own = [(at(r, 0), at(r + 1, 0)) for r in range(count - 1)] + [(at(r + 1, 1), at(r, 1)) for r in range(count - 1)]
    cross = [(at(r, 1), at(r + 1, 0)) for r in range(count - 1)] + [(at(r + 1, 0), at(r, 1)) for r in range(count - 1)]
    sent_own = jnp.where(me == 0, bottom, top)
    sent_cross = jnp.where(me == 0, top, bottom)
    axes = ("row", "chan")
    return lax.ppermute(sent_own, axes, own), lax.ppermute(sent_cross, axes, cross)


def facet_neighbours(wavelet_dual, reweight):
    axes = ("row", "chan")
    count = lax.axis_size(axes)
    up = [(i, i + 1) for i in range(count - 1)]
    down = [(j, i) for i, j in up]
    last = jnp.concatenate([wavelet_dual[:, -2:], reweight[None, -2:]])
    first = jnp.concatenate([wavelet_dual[:, :2], reweight[None, :2]])
    return lax.ppermute(last, axes, up), lax.ppermute(first, axes, down)


def per_device(sky_image, fourier_dual, visibilities, weights, radius, wavelet_dual, reweight):
    f32 = jnp.float32
    sky = sky_image[0]
    rows, length = sky.shape
    count = lax.axis_size("row")
    width = length // count
    per = width // count
    chunks = 2 if per % 2 == 0 else 1
    batch = width // chunks
    kept = per // chunks
    scale = 1.0 / math.sqrt(length)
    shape = jax.ShapeDtypeStruct

    any_space = pl.BlockSpec(memory_space=pl.ANY)
    dma = lambda n: pltpu.SemaphoreType.DMA((n,))
    n = count if count & (count - 1) == 0 and count <= 16 else 1
    pieces_of = lambda packed: [shape(packed[1:], f32)] * n if n > 1 else [shape(packed, f32)]

    def tile(high, wide):
        tiles, step = lane_tiles(wide)
        return tiles, high, step

    lanes = np.arange(width)
    tw = phase_rows(count, lanes, length)
    g_table = split_constant(scale * np.concatenate(dft_matrix(lanes, lanes, width, 1)))

    sent = []
    for c in range(chunks):
        picked = (np.arange(count)[:, None] * per + c * kept + np.arange(kept)[None, :]).reshape(-1)
        table = split_constant(scale * np.concatenate(dft_matrix(picked, lanes, width, 1)))
        args = (sky, *tw, *table)
        packed = (count, 2, *tile(batch, rows))
        piece = call(
            partial(first_kernel, count, width, kept, n), args,
            [any_space] + [whole(a.shape) for a in args[1:]], pieces_of(packed), [any_space] * n,
            [vmem(sky.shape), vmem(packed)] + [vmem((count, rows, width))] * 2 + [dma(SKY_PARTS), dma(n)],
            10**10, 10**7,
        )
        sent.append(row_exchange(piece))

    half = rows // 2
    me = lax.axis_index("chan")
    theirs = lax.dynamic_slice_in_dim(sky, (1 - me) * (half - 8), half + 8, 0)
    other = chan_swap(theirs)
    edge_own, edge_other = edges_of(sky)
    above, below = facet_neighbours(wavelet_dual, reweight)
    args = (sky, other, edge_own, edge_other, wavelet_dual, above, below, reweight)
    outs = (shape((2, half, length), f32), shape((2, 2, 8, length), f32))
    wavelet_new, outside = call(
        partial(wave_kernel, count), args, [any_space] * 4 + [whole(a.shape) for a in args[4:]],
        outs, tuple(whole(o.shape) for o in outs),
        [vmem((2, half + 16, length)), dma(4)], 10**10, 3 * 10**7,
    )
    outs = (shape((half, length), f32), shape((half, length), f32))
    adjoint_own, adjoint_other = call(
        adjoint_kernel, (wavelet_new, outside), [any_space] * 2, outs, tuple(whole(o.shape) for o in outs),
        [vmem((2, half + 16, length)), pltpu.SemaphoreType.DMA((2, 3))], 10**10, 3 * 10**7,
    )
    adjoint_got = chan_swap(adjoint_other)

    resid, returned, sums = [], [], np.zeros((2, 8, 128), np.float32)
    for c in range(chunks):
        block = lambda lead, c=c: pl.BlockSpec(
            (*lead, batch, length), lambda i: (0,) * len(lead) + (c, 0), pipeline_mode=pl.Buffered(1)
        )
        tables = (*tw, *g_table)
        coming = (count, 2, *tile(batch, rows))
        packed = (count, 2, *tile(rows, batch))
        outs = (shape((2, 1, batch, length), f32), shape((2, 8, 128), f32))
        d, part, *piece = call(
            partial(middle_kernel, count, width, n),
            (*sent[c], fourier_dual, visibilities, weights, sums, *tables),
            [any_space] * n + [block((2, 1)), block((2, 1)), block((1,)), *(whole(t.shape) for t in (sums, *tables))],
            [*outs, *pieces_of(packed)], [whole(o.shape) for o in outs] + [any_space] * n,
            [vmem(coming), vmem(packed)] + [vmem((count, batch, width))] * 2 + [vmem((-(-batch // 128), length, 128))] * 2 + [vmem((batch, length))] * 2 + [dma(n)],
            2 * 10**10, 3 * 10**7,
        )
        resid.append(d)
        sums = part
        returned.append(row_exchange(piece))

    total = row_total(sums) if n > 1 else lax.psum(sums, "row")
    data_norm = jnp.sum(total[1])
    resid_norm = jnp.sum(total[0])
    shrink = data_step * (1.0 - radius * jnp.sqrt(data_norm) / jnp.sqrt(resid_norm))
    fourier_new = jnp.concatenate([d * shrink for d in resid], axis=2)

    base = (sky, adjoint_own, adjoint_got)
    for c in range(chunks):
        packed = (count, 2, *tile(rows, batch))
        args = (*returned[c], *base, *tw, *g_table, shrink)
        specs = [any_space] * (n + len(base)) + [whole(a.shape) for a in (*tw, *g_table)]
        specs.append(pl.BlockSpec(memory_space=pltpu.SMEM))
        scratch = [
            vmem(packed), vmem((rows, length)), *[vmem((count, rows, batch))] * 2,
            vmem((-(-rows // 128), length, 128)), dma(7), dma(GOT_PARTS * n), *[vmem((rows, length))] * (c == 0),
        ]
        image_new = call(
            partial(last_kernel, count, width, c * batch, n, c == 0, c == chunks - 1), args, specs,
            shape((rows, length), f32), any_space, scratch, 10**10, 3 * 10**7,
        )
        base = (image_new,)
    return (image_new[None], fourier_new, wavelet_new)


def solution(mesh):
    in_specs = (
        P("chan", "row", None),
        P(None, "chan", "row", None),
        P(None, "chan", "row", None),
        P("chan", "row", None),
        P("chan"),
        P(None, ("row", "chan"), None),
        P(("row", "chan"), None),
    )
    out_specs = (
        P("chan", "row", None),
        P(None, "chan", "row", None),
        P(None, ("row", "chan"), None),
    )

    return jax.shard_map(per_device, mesh=mesh, in_specs=in_specs, out_specs=out_specs, check_vma=False)
```
